512 devices in a mesh: tm: 32 (over y, x), state: 16 (over z, core).
Axes of the slice: x: 4, y: 8, z: 8, core: 2. Of those that a mesh axis runs over, the one named last changes fastest.
Arguments:
- prior: float32 [1024], replicated, may hold values from -6 to 6
- transition: bfloat16 [1024, 1024], replicated, may hold values from -1 to 1, as said below
- gain: bfloat16 [1024, 1024], replicated, may hold values from -1 to 1, as said below
- smoother: bfloat16 [1024, 1024], P('state'), may hold values from -1 to 1, as said below
- observed: float32 [128, 1024], P('tm'), may hold values from -6 to 6
- present: int32 [128], P('tm'), may hold values 0 or 1
Outputs:
- filtered: float32 [128, 1024], P('tm', 'state')
- smoothed: float32 [128, 1024], P('tm', 'state')
The draws below stay inside these ranges and needn't reach their ends.
Inputs may be any that keep to these rules, and one draw needn't show every extreme that they name: transition: diagonal entries 1 - r with r log-uniform between 0.003 and 0.1 over the coefficients, plus an antisymmetric part whose entries have standard deviation about 0.1 / (2 sqrt(2048)) times sqrt(2). gain: diagonal entries log-uniform between 0.005 and 0.5, plus a symmetric part whose entries have standard deviation about 0.004 sqrt(2) / sqrt(1024). smoother: diagonal entries 1 - r with r log-uniform between 0.006 and 0.4, plus a symmetric part whose entries have standard deviation about 0.003 sqrt(2) / sqrt(1024); its spectral radius is below one.
All inputs are finite; a program needn't handle non-finite values. No bound on the sum of `present` on one device may be relied on, other than what follows from the above.
Results may differ from the reference program's by a relative error of at most 0.0003.
Values may be sent and summed in bfloat16 or wider, within the bound.
A program may use at most 128 MiB of HBM per device.

```python
import math
import jax
import jax.numpy as jnp
from jax import lax

N = 1024
STEPS = 128


def draw_transition(key, part):
    rate_key = jax.random.fold_in(key, 11)
    noise_seed_key = jax.random.fold_in(key, 12)
    damping_factors = jnp.exp(jax.random.uniform(rate_key, (N,), jnp.float32, math.log(0.003), math.log(0.1)))
    noise_draw = jax.random.normal(noise_seed_key, (N, N), jnp.float32)
    skew_part = (noise_draw - noise_draw.T) * (0.1 / (2.0 * math.sqrt(2.0 * N)))
    diagonal = jnp.eye(N, dtype=jnp.float32) * (1.0 - damping_factors)[None, :]
    return (diagonal + skew_part).astype(jnp.bfloat16)


def draw_gain(key, part):
    rate_key = jax.random.fold_in(key, 21)
    noise_seed_key = jax.random.fold_in(key, 22)
    gain_values = jnp.exp(jax.random.uniform(rate_key, (N,), jnp.float32, math.log(0.005), math.log(0.5)))
    noise_draw = jax.random.normal(noise_seed_key, (N, N), jnp.float32)
    symmetric = (noise_draw + noise_draw.T) * (0.004 / math.sqrt(N))
    diagonal = jnp.eye(N, dtype=jnp.float32) * gain_values[None, :]
    return (diagonal + symmetric).astype(jnp.bfloat16)


def draw_smoother(key, part):
    rate_key = jax.random.fold_in(key, 31)
    noise_seed_key = jax.random.fold_in(key, 32)
    damping_factors = jnp.exp(jax.random.uniform(rate_key, (N,), jnp.float32, math.log(0.006), math.log(0.4)))
    noise_draw = jax.random.normal(noise_seed_key, (N, N), jnp.float32)
    symmetric = (noise_draw + noise_draw.T) * (0.003 / math.sqrt(N))
    diagonal = jnp.eye(N, dtype=jnp.float32) * (1.0 - damping_factors)[None, :]
    return (diagonal + symmetric).astype(jnp.bfloat16)


def plant(drawn, rng, low, top_value):
    longest = drawn.shape.index(max(drawn.shape))
    spots = []
    for shift in (0, 1):
        where = [jax.random.randint(jax.random.fold_in(rng, axis), (), 0, length) for axis, length in enumerate(drawn.shape)]
        where[longest] = (where[longest] + shift) % drawn.shape[longest]
        spots.append(tuple(where))
    return drawn.at[spots[0]].set(low).at[spots[1]].set(top_value)


def block_scale(stream_key, shape, cuts, low, high):
    def one(dim, shards_of):
        steps = jax.random.uniform(jax.random.fold_in(jax.random.fold_in(stream_key, 6), dim), (shards_of,), jnp.float32, low / len(cuts), high / len(cuts))
        return jnp.repeat(jnp.exp(steps), shape[dim] // shards_of).reshape((-1,) + (1,) * (len(shape) - dim - 1))

    factor_of = one(*cuts[0])
    for cut in cuts[1:]:
        factor_of = factor_of * one(*cut)
    return factor_of


def centred(key, extent, width, reach, shards=(), held_as=jnp.bfloat16):
    entries = width * jax.random.normal(key, extent, jnp.float32)
    if shards:
        entries = entries * block_scale(key, extent, shards, -0.22, 0.18)
    return jnp.clip(entries, -reach, reach).astype(held_as)


def setup_inputs(seed: int = 0) -> dict:
    arg_keys = jax.random.split(jax.random.key(seed), 7)
    prior = centred(arg_keys[0], (N,), 1.0, 6.0, (), jnp.float32)
    transition = draw_transition(jax.random.fold_in(arg_keys[6], 71), 0)
    gain = draw_gain(jax.random.fold_in(arg_keys[6], 71), 0)
    smoother = draw_smoother(jax.random.fold_in(arg_keys[6], 71), 0)
    observed = centred(arg_keys[4], (STEPS, N), 1.0, 6.0, ((0, 32),), jnp.float32)
    present = plant((jax.random.randint(arg_keys[5], (STEPS,), 0, 2) < 1).astype(jnp.int32), jax.random.fold_in(arg_keys[5], 1), 0, 1)
    return {"prior": prior, "transition": transition, "gain": gain, "smoother": smoother, "observed": observed, "present": present}


HIGH_PRECISION = lax.Precision.HIGHEST


def reference(prior, transition, gain, smoother, observed, present):
    weights = present.astype(jnp.float32)

    def filter_step(state_vector, inputs):
        observation, weight = inputs
        predicted = jnp.dot(transition, state_vector, precision=HIGH_PRECISION)
        updated = predicted + weight * jnp.dot(gain, observation - predicted, precision=HIGH_PRECISION)
        return updated, updated

    _, filtered = lax.scan(filter_step, prior, (observed, weights))

    def smooth_step(next_vector, current):
        shifted = next_vector - jnp.dot(transition, current, precision=HIGH_PRECISION)
        value = current + jnp.dot(smoother, shifted, precision=HIGH_PRECISION)
        return value, value

    _, earlier_states = lax.scan(smooth_step, filtered[-1], filtered[:-1], reverse=True)
    smoothed = jnp.concatenate([earlier_states, filtered[-1:]], axis=0)
    return filtered, smoothed
```

```python
import functools

import jax
import jax.numpy as jnp
from jax import lax
from jax.experimental import pallas as pl
from jax.experimental.pallas import tpu as pltpu
from jax.sharding import PartitionSpec as P

F32 = jnp.float32
BF16 = jnp.bfloat16
NT = (((1,), (1,)), ((), ()))


def pieces(x):
    hi = x.astype(BF16)
    rest = x - hi.astype(F32)
    mid = rest.astype(BF16)
    lo = (rest - mid.astype(F32)).astype(BF16)
    return hi, mid, lo


def times_transpose(rows, matrix):
    total = None
    for part in pieces(rows):
        term = lax.dot_general(part, matrix, NT, preferred_element_type=F32)
        total = term if total is None else total + term
    return total


def matvec_row(vector, matrix):
    hi, mid, lo = pieces(vector)
    width = vector.shape[1]
    row = lax.broadcasted_iota(jnp.int32, (8, width), 0)
    stacked = jnp.where(
        row == 0,
        hi.astype(F32),
        jnp.where(row == 1, mid.astype(F32), jnp.where(row == 2, lo.astype(F32), 0.0)),
    ).astype(BF16)
    out = lax.dot_general(stacked, matrix, NT, preferred_element_type=F32)
    return out[0:1] + out[1:2] + out[2:3]


def chain_kernel(w_ref, prior_ref, a_ref, g_ref, s_ref, y_ref, f_ref, sm_ref, p_ref):
    steps = y_ref.shape[0]

    def filter_step(k, state):
        predicted = matvec_row(state, a_ref[...])
        innovation = y_ref[pl.ds(k, 1), :] - predicted
        updated = predicted + w_ref[k] * matvec_row(innovation, g_ref[...])
        f_ref[pl.ds(k, 1), :] = updated
        return updated

    last = lax.fori_loop(0, steps, filter_step, prior_ref[...])
    p_ref[...] = times_transpose(f_ref[...], a_ref[...])
    sm_ref[pl.ds(steps - 1, 1), :] = last

    def smooth_step(j, later):
        k = steps - 2 - j
        value = f_ref[pl.ds(k, 1), :] + matvec_row(later - p_ref[pl.ds(k, 1), :], s_ref[...])
        sm_ref[pl.ds(k, 1), :] = value
        return value

    lax.fori_loop(0, steps - 1, smooth_step, last)


def run_chain(weights, prior, transition, gain, smoother, observed):
    steps, width = observed.shape
    vmem = pl.BlockSpec(memory_space=pltpu.VMEM)
    smem = pl.BlockSpec(memory_space=pltpu.SMEM)
    full = jax.ShapeDtypeStruct((steps, width), F32)
    return pl.pallas_call(
        chain_kernel,
        out_shape=(full, full),
        in_specs=[smem, vmem, vmem, vmem, vmem, vmem],
        out_specs=(vmem, vmem),
        scratch_shapes=[pltpu.VMEM((steps, width), F32)],
        compiler_params=pltpu.CompilerParams(vmem_limit_bytes=48 * 1024 * 1024),
    )(weights, prior, transition, gain, smoother, observed)


def local(prior, transition, gain, smoother, observed, present):
    panel = smoother.shape[0]
    seg = observed.shape[0]
    all_observed = lax.all_gather(observed, "tm", axis=0, tiled=True)
    weights = lax.all_gather(present.astype(F32), "tm", axis=0, tiled=True)
    smoother_full = lax.all_gather(smoother, "state", axis=0, tiled=True)
    filtered, smoothed = run_chain(
        weights, prior[None, :], transition, gain, smoother_full, all_observed
    )
    t0 = lax.axis_index("tm") * seg
    c0 = lax.axis_index("state") * panel
    block = lambda full: lax.dynamic_slice(full, (t0, c0), (seg, panel))
    return block(filtered), block(smoothed)


def solution(mesh):
    placed = (P(), P(), P(), P("state", None), P("tm", None), P("tm"))
    return jax.shard_map(
        local,
        mesh=mesh,
        in_specs=placed,
        out_specs=(P("tm", "state"), P("tm", "state")),
        check_vma=False,
    )
```

```python
import functools

import jax
import jax.numpy as jnp
from jax import lax
from jax.experimental import pallas as pl
from jax.experimental.pallas import tpu as pltpu
from jax.sharding import PartitionSpec as P

F32 = jnp.float32
BF16 = jnp.bfloat16
NT = (((1,), (1,)), ((), ()))


def pieces(x):
    hi = x.astype(BF16)
    rest = x - hi.astype(F32)
    mid = rest.astype(BF16)
    lo = (rest - mid.astype(F32)).astype(BF16)
    return hi, mid, lo


def times_transpose(rows, matrix):
    total = None
    for part in pieces(rows):
        term = lax.dot_general(part, matrix, NT, preferred_element_type=F32)
        total = term if total is None else total + term
    return total


def matvec_row(vector, matrix):
    hi, mid, lo = pieces(vector)
    width = vector.shape[1]
    row = lax.broadcasted_iota(jnp.int32, (8, width), 0)
    stacked = jnp.where(
        row == 0,
        hi.astype(F32),
        jnp.where(row == 1, mid.astype(F32), jnp.where(row == 2, lo.astype(F32), 0.0)),
    ).astype(BF16)
    out = lax.dot_general(stacked, matrix, NT, preferred_element_type=F32)
    return out[0:1] + out[1:2] + out[2:3]


def filter_kernel(w_ref, prior_ref, a_ref, g_ref, y_ref, f_ref):
    steps = y_ref.shape[0]

    def filter_step(k, state):
        predicted = matvec_row(state, a_ref[...])
        innovation = y_ref[pl.ds(k, 1), :] - predicted
        updated = predicted + w_ref[k] * matvec_row(innovation, g_ref[...])
        f_ref[pl.ds(k, 1), :] = updated
        return updated

    lax.fori_loop(0, steps, filter_step, prior_ref[...])


def smooth_kernel(f_ref, a_ref, s_ref, sm_ref, p_ref):
    steps = f_ref.shape[0]
    p_ref[...] = times_transpose(f_ref[...], a_ref[...])
    last = f_ref[pl.ds(steps - 1, 1), :]
    sm_ref[pl.ds(steps - 1, 1), :] = last

    def smooth_step(j, later):
        k = steps - 2 - j
        value = f_ref[pl.ds(k, 1), :] + matvec_row(later - p_ref[pl.ds(k, 1), :], s_ref[...])
        sm_ref[pl.ds(k, 1), :] = value
        return value

    lax.fori_loop(0, steps - 1, smooth_step, last)


VMEM_LIMIT = 48 * 1024 * 1024


def run_filter(weights, prior, transition, gain, observed):
    vmem = pl.BlockSpec(memory_space=pltpu.VMEM)
    smem = pl.BlockSpec(memory_space=pltpu.SMEM)
    return pl.pallas_call(
        filter_kernel,
        out_shape=jax.ShapeDtypeStruct(observed.shape, F32),
        in_specs=[smem, vmem, vmem, vmem, vmem],
        out_specs=vmem,
        compiler_params=pltpu.CompilerParams(vmem_limit_bytes=VMEM_LIMIT),
    )(weights, prior, transition, gain, observed)


def run_smoother(filtered, transition, smoother):
    vmem = pl.BlockSpec(memory_space=pltpu.VMEM)
    return pl.pallas_call(
        smooth_kernel,
        out_shape=jax.ShapeDtypeStruct(filtered.shape, F32),
        in_specs=[vmem, vmem, vmem],
        out_specs=vmem,
        scratch_shapes=[pltpu.VMEM(filtered.shape, F32)],
        compiler_params=pltpu.CompilerParams(vmem_limit_bytes=VMEM_LIMIT),
    )(filtered, transition, smoother)


def run_chain(weights, prior, transition, gain, smoother, observed):
    filtered = run_filter(weights, prior, transition, gain, observed)
    return filtered, run_smoother(filtered, transition, smoother)


def gather_kernel(count, block_ref, out_ref, local_sem, send_sems, recv_sems):
    me = lax.axis_index("tm")
    mesh_id = pl.DeviceIdType.MESH
    barrier = pltpu.get_barrier_semaphore()
    for step in range(1, count):
        peer = lax.rem(me + step, count)
        pl.semaphore_signal(barrier, inc=1, device_id={"tm": peer}, device_id_type=mesh_id)
    pl.semaphore_wait(barrier, count - 1)
    own = pltpu.make_async_copy(block_ref, out_ref.at[me], local_sem)
    own.start()
    copies = []
    for step in range(1, count):
        peer = lax.rem(me + step, count)
        copy = pltpu.make_async_remote_copy(
            src_ref=block_ref,
            dst_ref=out_ref.at[me],
            send_sem=send_sems.at[step],
            recv_sem=recv_sems.at[step],
            device_id={"tm": peer},
            device_id_type=mesh_id,
        )
        copy.start()
        copies.append(copy)
    for copy in copies:
        copy.wait()
    own.wait()


def gather_over_time(block):
    count = lax.axis_size("tm")
    vmem = pl.BlockSpec(memory_space=pltpu.VMEM)
    return pl.pallas_call(
        functools.partial(gather_kernel, count),
        out_shape=jax.ShapeDtypeStruct((count,) + block.shape, block.dtype),
        in_specs=[vmem],
        out_specs=vmem,
        scratch_shapes=[
            pltpu.SemaphoreType.DMA,
            pltpu.SemaphoreType.DMA((count,)),
            pltpu.SemaphoreType.DMA((count,)),
        ],
        compiler_params=pltpu.CompilerParams(collective_id=0, has_side_effects=True),
    )(block)


def local(prior, transition, gain, smoother, observed, present):
    panel = smoother.shape[0]
    seg, width = observed.shape
    flags = jnp.broadcast_to(present.astype(F32)[:, None], (seg, 128))
    block = jnp.concatenate([observed, flags], axis=1)
    block = jnp.concatenate([block, jnp.zeros((8 - seg, width + 128), F32)], axis=0)
    slots = gather_over_time(block)
    all_observed = slots[:, :seg, :width].reshape(-1, width)
    weights = slots[:, :seg, width].reshape(-1)
    smoother_full = lax.all_gather(smoother, "state", axis=0, tiled=True)
    filtered, smoothed = run_chain(
        weights, prior[None, :], transition, gain, smoother_full, all_observed
    )
    t0 = lax.axis_index("tm") * seg
    c0 = lax.axis_index("state") * panel
    block_of = lambda full: lax.dynamic_slice(full, (t0, c0), (seg, panel))
    return block_of(filtered), block_of(smoothed)


def solution(mesh):
    placed = (P(), P(), P(), P("state", None), P("tm", None), P("tm"))
    return jax.shard_map(
        local,
        mesh=mesh,
        in_specs=placed,
        out_specs=(P("tm", "state"), P("tm", "state")),
        check_vma=False,
    )
```

```python
import functools

import jax
import jax.numpy as jnp
from jax import lax
from jax.experimental import pallas as pl
from jax.experimental.pallas import tpu as pltpu
from jax.sharding import PartitionSpec as P

F32 = jnp.float32
BF16 = jnp.bfloat16
NT = (((1,), (1,)), ((), ()))


def pieces(x):
    hi = x.astype(BF16)
    rest = x - hi.astype(F32)
    mid = rest.astype(BF16)
    lo = (rest - mid.astype(F32)).astype(BF16)
    return hi, mid, lo


def times_transpose(rows, matrix):
    total = None
    for part in pieces(rows):
        term = lax.dot_general(part, matrix, NT, preferred_element_type=F32)
        total = term if total is None else total + term
    return total


def matvec_row(vector, matrix):
    hi, mid, lo = pieces(vector)
    width = vector.shape[1]
    row = lax.broadcasted_iota(jnp.int32, (8, width), 0)
    stacked = jnp.where(
        row == 0,
        hi.astype(F32),
        jnp.where(row == 1, mid.astype(F32), jnp.where(row == 2, lo.astype(F32), 0.0)),
    ).astype(BF16)
    out = lax.dot_general(stacked, matrix, NT, preferred_element_type=F32)
    return out[0:1] + out[1:2] + out[2:3]


def column_from_row(matrix, row):
    return jnp.sum(matrix * row, axis=1, keepdims=True)


def row_from_column(matrix_t, column):
    return jnp.sum(matrix_t * column, axis=0, keepdims=True)


def filter_kernel(
    flag_ref, prior_ref, w_ref, y_ref, a_ref, g_ref, pair_ref, pair_t_ref,
    even_ref, odd_ref, extra_ref, prev_ref,
):
    half = y_ref.shape[1]
    gain = g_ref[...]
    transition = a_ref[...]
    w_even, w_odd = w_ref[0], w_ref[1]
    y_even, y_odd = y_ref[0], y_ref[1]
    corr_even = w_even * times_transpose(y_even, gain)
    corr_odd = w_odd * times_transpose(y_odd, gain)
    moved = times_transpose(corr_even, transition)
    extra_ref[...] = moved - w_odd * times_transpose(moved, gain) + corr_odd

    def pair_step(i, state):
        middle = column_from_row(pair_ref[flag_ref[2 * i]], state)
        updated = row_from_column(pair_t_ref[flag_ref[2 * i + 1]], middle)
        updated = updated + extra_ref[pl.ds(i, 1), :]
        odd_ref[pl.ds(i, 1), :] = updated
        return updated

    lax.fori_loop(0, half, pair_step, prior_ref[...])
    prev_ref[0:1, :] = prior_ref[...]
    prev_ref[1:half, :] = odd_ref[0 : half - 1, :]
    predicted = times_transpose(prev_ref[...], transition)
    even_ref[...] = predicted + w_even * times_transpose(y_even - predicted, gain)


def smooth_kernel(
    even_ref, odd_ref, a_ref, s_ref, s32_ref, s32_t_ref,
    s_even_ref, s_odd_ref, extra_ref, d_even_ref,
):
    half = even_ref.shape[0]
    smoother = s_ref[...]
    transition = a_ref[...]
    f_even, f_odd = even_ref[...], odd_ref[...]
    d_even_ref[...] = f_even - times_transpose(times_transpose(f_even, transition), smoother)
    d_odd = f_odd - times_transpose(times_transpose(f_odd, transition), smoother)
    pulled = times_transpose(d_even_ref[...], smoother)
    extra_ref[0 : half - 1, :] = pulled[1:half, :] + d_odd[0 : half - 1, :]
    last = odd_ref[half - 1 : half, :]
    s_odd_ref[half - 1 : half, :] = last

    def pair_step(j, state):
        r = half - 2 - j
        middle = column_from_row(s32_ref[...], state)
        value = row_from_column(s32_t_ref[...], middle) + extra_ref[pl.ds(r, 1), :]
        s_odd_ref[pl.ds(r, 1), :] = value
        return value

    lax.fori_loop(0, half - 1, pair_step, last)
    s_even_ref[...] = times_transpose(s_odd_ref[...], smoother) + d_even_ref[...]


VMEM_LIMIT = 60 * 1024 * 1024


def run_chain(weights, prior, transition, gain, smoother, observed):
    steps, width = observed.shape
    half = steps // 2
    vmem = pl.BlockSpec(memory_space=pltpu.VMEM)
    smem = pl.BlockSpec(memory_space=pltpu.SMEM)
    params = pltpu.CompilerParams(vmem_limit_bytes=VMEM_LIMIT)
    flags = weights.astype(jnp.int32)
    w_pair = weights.reshape(half, 2).T[:, :, None]
    y_pair = observed.reshape(half, 2, width).transpose(1, 0, 2)
    a32 = transition.astype(F32)
    b32 = a32 - jnp.dot(gain, transition, preferred_element_type=F32)
    pair = jnp.stack([a32, b32])
    pair_t = jnp.stack([a32.T, b32.T])
    rows = jax.ShapeDtypeStruct((half, width), F32)
    f_even, f_odd = pl.pallas_call(
        filter_kernel,
        out_shape=(rows, rows),
        in_specs=[smem] + [vmem] * 7,
        out_specs=(vmem, vmem),
        scratch_shapes=[pltpu.VMEM((half, width), F32)] * 2,
        compiler_params=params,
    )(flags, prior, w_pair, y_pair, transition, gain, pair, pair_t)
    s32 = smoother.astype(F32)
    s_even, s_odd = pl.pallas_call(
        smooth_kernel,
        out_shape=(rows, rows),
        in_specs=[vmem] * 6,
        out_specs=(vmem, vmem),
        scratch_shapes=[pltpu.VMEM((half, width), F32)] * 2,
        compiler_params=params,
    )(f_even, f_odd, transition, smoother, s32, s32.T)
    interleave = lambda even, odd: jnp.stack([even, odd], axis=1).reshape(steps, width)
    return interleave(f_even, f_odd), interleave(s_even, s_odd)


def gather_kernel(count, block_ref, out_ref, local_sem, send_sems, recv_sems):
    me = lax.axis_index("tm")
    mesh_id = pl.DeviceIdType.MESH
    barrier = pltpu.get_barrier_semaphore()
    for step in range(1, count):
        peer = lax.rem(me + step, count)
        pl.semaphore_signal(barrier, inc=1, device_id={"tm": peer}, device_id_type=mesh_id)
    pl.semaphore_wait(barrier, count - 1)
    own = pltpu.make_async_copy(block_ref, out_ref.at[me], local_sem)
    own.start()
    copies = []
    for step in range(1, count):
        peer = lax.rem(me + step, count)
        copy = pltpu.make_async_remote_copy(
            src_ref=block_ref,
            dst_ref=out_ref.at[me],
            send_sem=send_sems.at[step],
            recv_sem=recv_sems.at[step],
            device_id={"tm": peer},
            device_id_type=mesh_id,
        )
        copy.start()
        copies.append(copy)
    for copy in copies:
        copy.wait()
    own.wait()


def gather_over_time(block):
    count = lax.axis_size("tm")
    vmem = pl.BlockSpec(memory_space=pltpu.VMEM)
    return pl.pallas_call(
        functools.partial(gather_kernel, count),
        out_shape=jax.ShapeDtypeStruct((count,) + block.shape, block.dtype),
        in_specs=[vmem],
        out_specs=vmem,
        scratch_shapes=[
            pltpu.SemaphoreType.DMA,
            pltpu.SemaphoreType.DMA((count,)),
            pltpu.SemaphoreType.DMA((count,)),
        ],
        compiler_params=pltpu.CompilerParams(collective_id=0, has_side_effects=True),
    )(block)


def local(prior, transition, gain, smoother, observed, present):
    panel = smoother.shape[0]
    seg, width = observed.shape
    flags = jnp.broadcast_to(present.astype(F32)[:, None], (seg, 128))
    block = jnp.concatenate([observed, flags], axis=1)
    block = jnp.concatenate([block, jnp.zeros((8 - seg, width + 128), F32)], axis=0)
    slots = gather_over_time(block)
    all_observed = slots[:, :seg, :width].reshape(-1, width)
    weights = slots[:, :seg, width].reshape(-1)
    smoother_full = lax.all_gather(smoother, "state", axis=0, tiled=True)
    filtered, smoothed = run_chain(
        weights, prior[None, :], transition, gain, smoother_full, all_observed
    )
    t0 = lax.axis_index("tm") * seg
    c0 = lax.axis_index("state") * panel
    block_of = lambda full: lax.dynamic_slice(full, (t0, c0), (seg, panel))
    return block_of(filtered), block_of(smoothed)


def solution(mesh):
    placed = (P(), P(), P(), P("state", None), P("tm", None), P("tm"))
    return jax.shard_map(
        local,
        mesh=mesh,
        in_specs=placed,
        out_specs=(P("tm", "state"), P("tm", "state")),
        check_vma=False,
    )
```

```python
import functools

import jax
import jax.numpy as jnp
from jax import lax
from jax.experimental import pallas as pl
from jax.experimental.pallas import tpu as pltpu
from jax.sharding import PartitionSpec as P

F32 = jnp.float32
BF16 = jnp.bfloat16
NT = (((1,), (1,)), ((), ()))


def pieces(x):
    hi = x.astype(BF16)
    rest = x - hi.astype(F32)
    mid = rest.astype(BF16)
    lo = (rest - mid.astype(F32)).astype(BF16)
    return hi, mid, lo


def times_transpose(rows, matrix):
    total = None
    for part in pieces(rows):
        term = lax.dot_general(part, matrix, NT, preferred_element_type=F32)
        total = term if total is None else total + term
    return total


def matvec_row(vector, matrix):
    hi, mid, lo = pieces(vector)
    width = vector.shape[1]
    row = lax.broadcasted_iota(jnp.int32, (8, width), 0)
    stacked = jnp.where(
        row == 0,
        hi.astype(F32),
        jnp.where(row == 1, mid.astype(F32), jnp.where(row == 2, lo.astype(F32), 0.0)),
    ).astype(BF16)
    out = lax.dot_general(stacked, matrix, NT, preferred_element_type=F32)
    return out[0:1] + out[1:2] + out[2:3]


def column_from_row(matrix, row):
    return jnp.sum(matrix * row, axis=1, keepdims=True)


def row_from_column(matrix_t, column):
    return jnp.sum(matrix_t * column, axis=0, keepdims=True)


BAND = 256


def build_pairs(a_ref, g_ref, a_t_ref, g_t_ref, pair_ref, pair_t_ref):
    width = a_ref.shape[0]
    for start in range(0, width, BAND):
        rows = slice(start, start + BAND)
        a_rows = a_ref[rows, :].astype(F32)
        pair_ref[0, rows, :] = a_rows
        pair_ref[1, rows, :] = a_rows - jnp.dot(
            g_ref[rows, :], a_ref[...], preferred_element_type=F32
        )
        a_t_rows = a_t_ref[rows, :].astype(F32)
        pair_t_ref[0, rows, :] = a_t_rows
        pair_t_ref[1, rows, :] = a_t_rows - jnp.dot(
            a_t_ref[rows, :], g_t_ref[...], preferred_element_type=F32
        )


def filter_kernel(
    flag_ref, prior_ref, w_ref, y_ref, a_ref, g_ref, a_t_ref, g_t_ref,
    even_ref, odd_ref, extra_ref, prev_ref, pair_ref, pair_t_ref,
):
    half = y_ref.shape[1]
    build_pairs(a_ref, g_ref, a_t_ref, g_t_ref, pair_ref, pair_t_ref)
    gain = g_ref[...]
    transition = a_ref[...]
    w_even, w_odd = w_ref[0], w_ref[1]
    y_even, y_odd = y_ref[0], y_ref[1]
    corr_even = w_even * times_transpose(y_even, gain)
    corr_odd = w_odd * times_transpose(y_odd, gain)
    moved = times_transpose(corr_even, transition)
    extra_ref[...] = moved - w_odd * times_transpose(moved, gain) + corr_odd

    def pair_step(i, state):
        middle = column_from_row(pair_ref[flag_ref[2 * i]], state)
        updated = row_from_column(pair_t_ref[flag_ref[2 * i + 1]], middle)
        updated = updated + extra_ref[pl.ds(i, 1), :]
        odd_ref[pl.ds(i, 1), :] = updated
        return updated

    lax.fori_loop(0, half, pair_step, prior_ref[...])
    prev_ref[0:1, :] = prior_ref[...]
    prev_ref[1:half, :] = odd_ref[0 : half - 1, :]
    predicted = times_transpose(prev_ref[...], transition)
    even_ref[...] = predicted + w_even * times_transpose(y_even - predicted, gain)


def smooth_kernel(
    even_ref, odd_ref, a_ref, s_ref, s_t_ref,
    s_even_ref, s_odd_ref, extra_ref, d_even_ref, s32_ref, s32_t_ref,
):
    half = even_ref.shape[0]
    width = s_ref.shape[0]
    for start in range(0, width, BAND):
        rows = slice(start, start + BAND)
        s32_ref[rows, :] = s_ref[rows, :].astype(F32)
        s32_t_ref[rows, :] = s_t_ref[rows, :].astype(F32)
    smoother = s_ref[...]
    transition = a_ref[...]
    f_even, f_odd = even_ref[...], odd_ref[...]
    d_even_ref[...] = f_even - times_transpose(times_transpose(f_even, transition), smoother)
    d_odd = f_odd - times_transpose(times_transpose(f_odd, transition), smoother)
    pulled = times_transpose(d_even_ref[...], smoother)
    extra_ref[0 : half - 1, :] = pulled[1:half, :] + d_odd[0 : half - 1, :]
    last = odd_ref[half - 1 : half, :]
    s_odd_ref[half - 1 : half, :] = last

    def pair_step(j, state):
        r = half - 2 - j
        middle = column_from_row(s32_ref[...], state)
        value = row_from_column(s32_t_ref[...], middle) + extra_ref[pl.ds(r, 1), :]
        s_odd_ref[pl.ds(r, 1), :] = value
        return value

    lax.fori_loop(0, half - 1, pair_step, last)
    s_even_ref[...] = times_transpose(s_odd_ref[...], smoother) + d_even_ref[...]


VMEM_LIMIT = 60 * 1024 * 1024


def run_chain(weights, prior, transition, gain, smoother, observed):
    steps, width = observed.shape
    half = steps // 2
    vmem = pl.BlockSpec(memory_space=pltpu.VMEM)
    smem = pl.BlockSpec(memory_space=pltpu.SMEM)
    params = pltpu.CompilerParams(vmem_limit_bytes=VMEM_LIMIT)
    flags = weights.astype(jnp.int32)
    w_pair = weights.reshape(half, 2).T[:, :, None]
    y_pair = observed.reshape(half, 2, width).transpose(1, 0, 2)
    rows = jax.ShapeDtypeStruct((half, width), F32)
    square = pltpu.VMEM((width, width), F32)
    stacked = pltpu.VMEM((2, width, width), F32)
    f_even, f_odd = pl.pallas_call(
        filter_kernel,
        out_shape=(rows, rows),
        in_specs=[smem] + [vmem] * 7,
        out_specs=(vmem, vmem),
        scratch_shapes=[pltpu.VMEM((half, width), F32)] * 2 + [stacked, stacked],
        compiler_params=params,
    )(flags, prior, w_pair, y_pair, transition, gain, transition.T, gain.T)
    s_even, s_odd = pl.pallas_call(
        smooth_kernel,
        out_shape=(rows, rows),
        in_specs=[vmem] * 5,
        out_specs=(vmem, vmem),
        scratch_shapes=[pltpu.VMEM((half, width), F32)] * 2 + [square, square],
        compiler_params=params,
    )(f_even, f_odd, transition, smoother, smoother.T)
    interleave = lambda even, odd: jnp.stack([even, odd], axis=1).reshape(steps, width)
    return interleave(f_even, f_odd), interleave(s_even, s_odd)


def gather_kernel(count, block_ref, out_ref, local_sem, send_sems, recv_sems):
    me = lax.axis_index("tm")
    mesh_id = pl.DeviceIdType.MESH
    barrier = pltpu.get_barrier_semaphore()
    for step in range(1, count):
        peer = lax.rem(me + step, count)
        pl.semaphore_signal(barrier, inc=1, device_id={"tm": peer}, device_id_type=mesh_id)
    pl.semaphore_wait(barrier, count - 1)
    own = pltpu.make_async_copy(block_ref, out_ref.at[me], local_sem)
    own.start()
    copies = []
    for step in range(1, count):
        peer = lax.rem(me + step, count)
        copy = pltpu.make_async_remote_copy(
            src_ref=block_ref,
            dst_ref=out_ref.at[me],
            send_sem=send_sems.at[step],
            recv_sem=recv_sems.at[step],
            device_id={"tm": peer},
            device_id_type=mesh_id,
        )
        copy.start()
        copies.append(copy)
    for copy in copies:
        copy.wait()
    own.wait()


def gather_over_time(block):
    count = lax.axis_size("tm")
    vmem = pl.BlockSpec(memory_space=pltpu.VMEM)
    return pl.pallas_call(
        functools.partial(gather_kernel, count),
        out_shape=jax.ShapeDtypeStruct((count,) + block.shape, block.dtype),
        in_specs=[vmem],
        out_specs=vmem,
        scratch_shapes=[
            pltpu.SemaphoreType.DMA,
            pltpu.SemaphoreType.DMA((count,)),
            pltpu.SemaphoreType.DMA((count,)),
        ],
        compiler_params=pltpu.CompilerParams(collective_id=0, has_side_effects=True),
    )(block)


def local(prior, transition, gain, smoother, observed, present):
    panel = smoother.shape[0]
    seg, width = observed.shape
    flags = jnp.broadcast_to(present.astype(F32)[:, None], (seg, 128))
    block = jnp.concatenate([observed, flags], axis=1)
    block = jnp.concatenate([block, jnp.zeros((8 - seg, width + 128), F32)], axis=0)
    slots = gather_over_time(block)
    all_observed = slots[:, :seg, :width].reshape(-1, width)
    weights = slots[:, :seg, width].reshape(-1)
    smoother_full = lax.all_gather(smoother, "state", axis=0, tiled=True)
    filtered, smoothed = run_chain(
        weights, prior[None, :], transition, gain, smoother_full, all_observed
    )
    t0 = lax.axis_index("tm") * seg
    c0 = lax.axis_index("state") * panel
    block_of = lambda full: lax.dynamic_slice(full, (t0, c0), (seg, panel))
    return block_of(filtered), block_of(smoothed)


def solution(mesh):
    placed = (P(), P(), P(), P("state", None), P("tm", None), P("tm"))
    return jax.shard_map(
        local,
        mesh=mesh,
        in_specs=placed,
        out_specs=(P("tm", "state"), P("tm", "state")),
        check_vma=False,
    )
```

```python
import functools

import jax
import jax.numpy as jnp
from jax import lax
from jax.experimental import pallas as pl
from jax.experimental.pallas import tpu as pltpu
from jax.sharding import PartitionSpec as P

F32 = jnp.float32
BF16 = jnp.bfloat16
NT = (((1,), (1,)), ((), ()))


def pieces(x):
    hi = x.astype(BF16)
    rest = x - hi.astype(F32)
    mid = rest.astype(BF16)
    lo = (rest - mid.astype(F32)).astype(BF16)
    return hi, mid, lo


def times_transpose(rows, matrix):
    total = None
    for part in pieces(rows):
        term = lax.dot_general(part, matrix, NT, preferred_element_type=F32)
        total = term if total is None else total + term
    return total


def matvec_row(vector, matrix):
    hi, mid, lo = pieces(vector)
    width = vector.shape[1]
    row = lax.broadcasted_iota(jnp.int32, (8, width), 0)
    stacked = jnp.where(
        row == 0,
        hi.astype(F32),
        jnp.where(row == 1, mid.astype(F32), jnp.where(row == 2, lo.astype(F32), 0.0)),
    ).astype(BF16)
    out = lax.dot_general(stacked, matrix, NT, preferred_element_type=F32)
    return out[0:1] + out[1:2] + out[2:3]


def column_from_row(matrix, row):
    return jnp.sum(matrix * row, axis=1, keepdims=True)


def row_from_column(matrix_t, column):
    return jnp.sum(matrix_t * column, axis=0, keepdims=True)


BAND = 256


def transpose_into(dst, src):
    width = src.shape[0]
    for i in range(0, width, BAND):
        for j in range(0, width, BAND):
            dst[j : j + BAND, i : i + BAND] = src[i : i + BAND, j : j + BAND].T


def build_pairs(a_ref, g_ref, pair_ref, pair_t_ref):
    width = a_ref.shape[0]
    for start in range(0, width, BAND):
        rows = slice(start, start + BAND)
        a_rows = a_ref[rows, :].astype(F32)
        pair_ref[0, rows, :] = a_rows
        pair_ref[1, rows, :] = a_rows - jnp.dot(
            g_ref[rows, :], a_ref[...], preferred_element_type=F32
        )
    transpose_into(pair_t_ref.at[0], pair_ref.at[0])
    transpose_into(pair_t_ref.at[1], pair_ref.at[1])


def filter_kernel(
    flag_ref, prior_ref, w_ref, y_ref, a_ref, g_ref,
    even_ref, odd_ref, extra_ref, prev_ref, pair_ref, pair_t_ref,
):
    half = y_ref.shape[1]
    build_pairs(a_ref, g_ref, pair_ref, pair_t_ref)
    gain = g_ref[...]
    transition = a_ref[...]
    w_even, w_odd = w_ref[0], w_ref[1]
    y_even, y_odd = y_ref[0], y_ref[1]
    corr_even = w_even * times_transpose(y_even, gain)
    corr_odd = w_odd * times_transpose(y_odd, gain)
    moved = times_transpose(corr_even, transition)
    extra_ref[...] = moved - w_odd * times_transpose(moved, gain) + corr_odd

    def pair_step(i, state):
        middle = column_from_row(pair_ref[flag_ref[2 * i]], state)
        updated = row_from_column(pair_t_ref[flag_ref[2 * i + 1]], middle)
        updated = updated + extra_ref[pl.ds(i, 1), :]
        odd_ref[pl.ds(i, 1), :] = updated
        return updated

    lax.fori_loop(0, half, pair_step, prior_ref[...])
    prev_ref[0:1, :] = prior_ref[...]
    prev_ref[1:half, :] = odd_ref[0 : half - 1, :]
    predicted = times_transpose(prev_ref[...], transition)
    even_ref[...] = predicted + w_even * times_transpose(y_even - predicted, gain)


def smooth_kernel(
    even_ref, odd_ref, a_ref, s_ref,
    s_even_ref, s_odd_ref, extra_ref, d_even_ref, s32_ref, s32_t_ref,
):
    half = even_ref.shape[0]
    width = s_ref.shape[0]
    for start in range(0, width, BAND):
        rows = slice(start, start + BAND)
        s32_ref[rows, :] = s_ref[rows, :].astype(F32)
    transpose_into(s32_t_ref, s32_ref)
    smoother = s_ref[...]
    transition = a_ref[...]
    f_even, f_odd = even_ref[...], odd_ref[...]
    d_even_ref[...] = f_even - times_transpose(times_transpose(f_even, transition), smoother)
    d_odd = f_odd - times_transpose(times_transpose(f_odd, transition), smoother)
    pulled = times_transpose(d_even_ref[...], smoother)
    extra_ref[0 : half - 1, :] = pulled[1:half, :] + d_odd[0 : half - 1, :]
    last = odd_ref[half - 1 : half, :]
    s_odd_ref[half - 1 : half, :] = last

    def pair_step(j, state):
        r = half - 2 - j
        middle = column_from_row(s32_ref[...], state)
        value = row_from_column(s32_t_ref[...], middle) + extra_ref[pl.ds(r, 1), :]
        s_odd_ref[pl.ds(r, 1), :] = value
        return value

    lax.fori_loop(0, half - 1, pair_step, last)
    s_even_ref[...] = times_transpose(s_odd_ref[...], smoother) + d_even_ref[...]


VMEM_LIMIT = 60 * 1024 * 1024


def run_chain(weights, prior, transition, gain, smoother, observed):
    steps, width = observed.shape
    half = steps // 2
    vmem = pl.BlockSpec(memory_space=pltpu.VMEM)
    smem = pl.BlockSpec(memory_space=pltpu.SMEM)
    params = pltpu.CompilerParams(vmem_limit_bytes=VMEM_LIMIT)
    flags = weights.astype(jnp.int32)
    w_pair = weights.reshape(half, 2).T[:, :, None]
    y_pair = observed.reshape(half, 2, width).transpose(1, 0, 2)
    rows = jax.ShapeDtypeStruct((half, width), F32)
    square = pltpu.VMEM((width, width), F32)
    stacked = pltpu.VMEM((2, width, width), F32)
    f_even, f_odd = pl.pallas_call(
        filter_kernel,
        out_shape=(rows, rows),
        in_specs=[smem] + [vmem] * 5,
        out_specs=(vmem, vmem),
        scratch_shapes=[pltpu.VMEM((half, width), F32)] * 2 + [stacked, stacked],
        compiler_params=params,
    )(flags, prior, w_pair, y_pair, transition, gain)
    s_even, s_odd = pl.pallas_call(
        smooth_kernel,
        out_shape=(rows, rows),
        in_specs=[vmem] * 4,
        out_specs=(vmem, vmem),
        scratch_shapes=[pltpu.VMEM((half, width), F32)] * 2 + [square, square],
        compiler_params=params,
    )(f_even, f_odd, transition, smoother)
    interleave = lambda even, odd: jnp.stack([even, odd], axis=1).reshape(steps, width)
    return interleave(f_even, f_odd), interleave(s_even, s_odd)


def gather_kernel(count, block_ref, out_ref, local_sem, send_sems, recv_sems):
    me = lax.axis_index("tm")
    mesh_id = pl.DeviceIdType.MESH
    barrier = pltpu.get_barrier_semaphore()
    for step in range(1, count):
        peer = lax.rem(me + step, count)
        pl.semaphore_signal(barrier, inc=1, device_id={"tm": peer}, device_id_type=mesh_id)
    pl.semaphore_wait(barrier, count - 1)
    own = pltpu.make_async_copy(block_ref, out_ref.at[me], local_sem)
    own.start()
    copies = []
    for step in range(1, count):
        peer = lax.rem(me + step, count)
        copy = pltpu.make_async_remote_copy(
            src_ref=block_ref,
            dst_ref=out_ref.at[me],
            send_sem=send_sems.at[step],
            recv_sem=recv_sems.at[step],
            device_id={"tm": peer},
            device_id_type=mesh_id,
        )
        copy.start()
        copies.append(copy)
    for copy in copies:
        copy.wait()
    own.wait()


def gather_over_time(block):
    count = lax.axis_size("tm")
    vmem = pl.BlockSpec(memory_space=pltpu.VMEM)
    return pl.pallas_call(
        functools.partial(gather_kernel, count),
        out_shape=jax.ShapeDtypeStruct((count,) + block.shape, block.dtype),
        in_specs=[vmem],
        out_specs=vmem,
        scratch_shapes=[
            pltpu.SemaphoreType.DMA,
            pltpu.SemaphoreType.DMA((count,)),
            pltpu.SemaphoreType.DMA((count,)),
        ],
        compiler_params=pltpu.CompilerParams(collective_id=0, has_side_effects=True),
    )(block)


def local(prior, transition, gain, smoother, observed, present):
    panel = smoother.shape[0]
    seg, width = observed.shape
    dense = seg * width // 128
    flags = jnp.zeros((8, 128), F32).at[0, :seg].set(present.astype(F32))
    block = jnp.concatenate([observed.reshape(dense, 128), flags], axis=0)
    slots = gather_over_time(block)
    all_observed = slots[:, :dense, :].reshape(-1, width)
    weights = slots[:, dense, :seg].reshape(-1)
    smoother_full = lax.all_gather(smoother, "state", axis=0, tiled=True)
    filtered, smoothed = run_chain(
        weights, prior[None, :], transition, gain, smoother_full, all_observed
    )
    t0 = lax.axis_index("tm") * seg
    c0 = lax.axis_index("state") * panel
    block_of = lambda full: lax.dynamic_slice(full, (t0, c0), (seg, panel))
    return block_of(filtered), block_of(smoothed)


def solution(mesh):
    placed = (P(), P(), P(), P("state", None), P("tm", None), P("tm"))
    return jax.shard_map(
        local,
        mesh=mesh,
        in_specs=placed,
        out_specs=(P("tm", "state"), P("tm", "state")),
        check_vma=False,
    )
```

```python
import functools

import jax
import jax.numpy as jnp
from jax import lax
from jax.experimental import pallas as pl
from jax.experimental.pallas import tpu as pltpu
from jax.sharding import PartitionSpec as P

F32 = jnp.float32
BF16 = jnp.bfloat16
NT = (((1,), (1,)), ((), ()))


def pieces(x):
    hi = x.astype(BF16)
    rest = x - hi.astype(F32)
    mid = rest.astype(BF16)
    lo = (rest - mid.astype(F32)).astype(BF16)
    return hi, mid, lo


def times_transpose(rows, matrix):
    total = None
    for part in pieces(rows):
        term = lax.dot_general(part, matrix, NT, preferred_element_type=F32)
        total = term if total is None else total + term
    return total


def matvec_row(vector, matrix):
    hi, mid, lo = pieces(vector)
    width = vector.shape[1]
    row = lax.broadcasted_iota(jnp.int32, (8, width), 0)
    stacked = jnp.where(
        row == 0,
        hi.astype(F32),
        jnp.where(row == 1, mid.astype(F32), jnp.where(row == 2, lo.astype(F32), 0.0)),
    ).astype(BF16)
    out = lax.dot_general(stacked, matrix, NT, preferred_element_type=F32)
    return out[0:1] + out[1:2] + out[2:3]


def column_from_row(matrix, row):
    return jnp.sum(matrix * row, axis=1, keepdims=True)


def row_from_column(matrix_t, column):
    return jnp.sum(matrix_t * column, axis=0, keepdims=True)


BAND = 256


def transpose_into(dst, src):
    width = src.shape[0]
    for i in range(0, width, BAND):
        for j in range(0, width, BAND):
            dst[j : j + BAND, i : i + BAND] = src[i : i + BAND, j : j + BAND].T


def build_pairs(a_ref, g_ref, pair_ref, pair_t_ref):
    width = a_ref.shape[0]
    for start in range(0, width, BAND):
        rows = slice(start, start + BAND)
        a_rows = a_ref[rows, :].astype(F32)
        pair_ref[0, rows, :] = a_rows
        pair_ref[1, rows, :] = a_rows - jnp.dot(
            g_ref[rows, :], a_ref[...], preferred_element_type=F32
        )
    transpose_into(pair_t_ref.at[0], pair_ref.at[0])
    transpose_into(pair_t_ref.at[1], pair_ref.at[1])


def filter_kernel(
    flag_ref, prior_ref, w_ref, y_ref, a_ref, g_ref,
    even_ref, odd_ref, extra_ref, prev_ref, pair_ref, pair_t_ref,
):
    half = y_ref.shape[1]
    build_pairs(a_ref, g_ref, pair_ref, pair_t_ref)
    gain = g_ref[...]
    transition = a_ref[...]
    w_even, w_odd = w_ref[0], w_ref[1]
    y_even, y_odd = y_ref[0], y_ref[1]
    corr_even = w_even * times_transpose(y_even, gain)
    corr_odd = w_odd * times_transpose(y_odd, gain)
    moved = times_transpose(corr_even, transition)
    extra_ref[...] = moved - w_odd * times_transpose(moved, gain) + corr_odd

    def pair_step(i, state):
        middle = column_from_row(pair_ref[flag_ref[2 * i]], state)
        updated = row_from_column(pair_t_ref[flag_ref[2 * i + 1]], middle)
        updated = updated + extra_ref[pl.ds(i, 1), :]
        odd_ref[pl.ds(i, 1), :] = updated
        return updated

    lax.fori_loop(0, half, pair_step, prior_ref[...])
    prev_ref[0:1, :] = prior_ref[...]
    prev_ref[1:half, :] = odd_ref[0 : half - 1, :]
    predicted = times_transpose(prev_ref[...], transition)
    even_ref[...] = predicted + w_even * times_transpose(y_even - predicted, gain)


def smooth_kernel(
    even_ref, odd_ref, a_ref, s_ref,
    s_even_ref, s_odd_ref, extra_ref, d_even_ref, s32_ref, s32_t_ref,
):
    half = even_ref.shape[0]
    width = s_ref.shape[0]
    for start in range(0, width, BAND):
        rows = slice(start, start + BAND)
        s32_ref[rows, :] = s_ref[rows, :].astype(F32)
    transpose_into(s32_t_ref, s32_ref)
    smoother = s_ref[...]
    transition = a_ref[...]
    f_even, f_odd = even_ref[...], odd_ref[...]
    d_even_ref[...] = f_even - times_transpose(times_transpose(f_even, transition), smoother)
    d_odd = f_odd - times_transpose(times_transpose(f_odd, transition), smoother)
    pulled = times_transpose(d_even_ref[...], smoother)
    extra_ref[0 : half - 1, :] = pulled[1:half, :] + d_odd[0 : half - 1, :]
    last = odd_ref[half - 1 : half, :]
    s_odd_ref[half - 1 : half, :] = last

    def pair_step(j, state):
        r = half - 2 - j
        middle = column_from_row(s32_ref[...], state)
        value = row_from_column(s32_t_ref[...], middle) + extra_ref[pl.ds(r, 1), :]
        s_odd_ref[pl.ds(r, 1), :] = value
        return value

    lax.fori_loop(0, half - 1, pair_step, last)
    s_even_ref[...] = times_transpose(s_odd_ref[...], smoother) + d_even_ref[...]


VMEM_LIMIT = 60 * 1024 * 1024


def run_chain(weights, prior, transition, gain, smoother, observed):
    steps, width = observed.shape
    half = steps // 2
    vmem = pl.BlockSpec(memory_space=pltpu.VMEM)
    smem = pl.BlockSpec(memory_space=pltpu.SMEM)
    params = pltpu.CompilerParams(vmem_limit_bytes=VMEM_LIMIT)
    flags = weights.astype(jnp.int32)
    w_pair = weights.reshape(half, 2).T[:, :, None]
    y_pair = observed.reshape(half, 2, width).transpose(1, 0, 2)
    rows = jax.ShapeDtypeStruct((half, width), F32)
    square = pltpu.VMEM((width, width), F32)
    stacked = pltpu.VMEM((2, width, width), F32)
    f_even, f_odd = pl.pallas_call(
        filter_kernel,
        out_shape=(rows, rows),
        in_specs=[smem] + [vmem] * 5,
        out_specs=(vmem, vmem),
        scratch_shapes=[pltpu.VMEM((half, width), F32)] * 2 + [stacked, stacked],
        compiler_params=params,
    )(flags, prior, w_pair, y_pair, transition, gain)
    s_even, s_odd = pl.pallas_call(
        smooth_kernel,
        out_shape=(rows, rows),
        in_specs=[vmem] * 4,
        out_specs=(vmem, vmem),
        scratch_shapes=[pltpu.VMEM((half, width), F32)] * 2 + [square, square],
        compiler_params=params,
    )(f_even, f_odd, transition, smoother)
    return (f_even, f_odd), (s_even, s_odd)


def gather_kernel(count, block_ref, out_ref, local_sem, send_sems, recv_sems, swap_sems):
    me = lax.axis_index("tm")
    lane = lax.axis_index("state")
    core = lax.rem(lane, 2)
    sibling = lane + 1 - 2 * core
    half = count // 2
    share = half - 1
    mesh_id = pl.DeviceIdType.MESH
    barrier = pltpu.get_barrier_semaphore()
    for step in range(1, count):
        peer = lax.rem(me + step, count)
        pl.semaphore_signal(barrier, inc=1, device_id={"tm": peer}, device_id_type=mesh_id)
    pl.semaphore_signal(barrier, inc=1, device_id={"state": sibling}, device_id_type=mesh_id)
    pl.semaphore_wait(barrier, count)

    def fetch(step):
        peer = lax.rem(me + step, count)
        return pltpu.make_async_remote_copy(
            src_ref=block_ref,
            dst_ref=out_ref.at[step],
            send_sem=send_sems.at[step],
            recv_sem=recv_sems.at[step],
            device_id={"tm": peer},
            device_id_type=mesh_id,
        )

    own = pltpu.make_async_copy(block_ref, out_ref.at[0], local_sem)

    @pl.when(core == 0)
    def _():
        own.start()

    copies = [fetch(core * share + j + 1) for j in range(share)]
    for copy in copies:
        copy.start()
    last = fetch(count - 1)

    @pl.when(core == 1)
    def _():
        last.start()

    for copy in copies:
        copy.wait()

    @pl.when(core == 1)
    def _():
        last.wait()

    @pl.when(core == 0)
    def _():
        own.wait()

    mine = pl.ds(core * half, half)
    swap = pltpu.make_async_remote_copy(
        src_ref=out_ref.at[mine],
        dst_ref=out_ref.at[mine],
        send_sem=swap_sems.at[0],
        recv_sem=swap_sems.at[1],
        device_id={"state": sibling},
        device_id_type=mesh_id,
    )
    swap.start()
    swap.wait()


def gather_over_time(block):
    count = lax.axis_size("tm")
    vmem = pl.BlockSpec(memory_space=pltpu.VMEM)
    return pl.pallas_call(
        functools.partial(gather_kernel, count),
        out_shape=jax.ShapeDtypeStruct((count,) + block.shape, block.dtype),
        in_specs=[vmem],
        out_specs=vmem,
        scratch_shapes=[
            pltpu.SemaphoreType.DMA,
            pltpu.SemaphoreType.DMA((count,)),
            pltpu.SemaphoreType.DMA((count,)),
            pltpu.SemaphoreType.DMA((2,)),
        ],
        compiler_params=pltpu.CompilerParams(collective_id=0, has_side_effects=True),
    )(block)


def local(prior, transition, gain, smoother, observed, present):
    panel = smoother.shape[0]
    seg, width = observed.shape
    count = lax.axis_size("tm")
    me = lax.axis_index("tm")
    dense = seg * width // 128
    flags = jnp.zeros((8, 128), F32).at[0, :seg].set(present.astype(F32))
    block = jnp.concatenate([observed.reshape(dense, 128), flags], axis=0)
    slots = gather_over_time(block)
    order = lax.rem(me - jnp.arange(count) + count, count)
    slots = jnp.take(slots, order, axis=0)
    all_observed = slots[:, :dense, :].reshape(-1, width)
    weights = slots[:, dense, :seg].reshape(-1)
    smoother_full = lax.all_gather(smoother, "state", axis=0, tiled=True)
    (f_even, f_odd), (s_even, s_odd) = run_chain(
        weights, prior[None, :], transition, gain, smoother_full, all_observed
    )
    r0 = me * (seg // 2)
    c0 = lax.axis_index("state") * panel

    def block_of(even, odd):
        pick = lambda rows: lax.dynamic_slice(rows, (r0, c0), (seg // 2, panel))
        return jnp.stack([pick(even), pick(odd)], axis=1).reshape(seg, panel)

    return block_of(f_even, f_odd), block_of(s_even, s_odd)


def solution(mesh):
    placed = (P(), P(), P(), P("state", None), P("tm", None), P("tm"))
    return jax.shard_map(
        local,
        mesh=mesh,
        in_specs=placed,
        out_specs=(P("tm", "state"), P("tm", "state")),
        check_vma=False,
    )
```

```python
import functools

import jax
import jax.numpy as jnp
from jax import lax
from jax.experimental import pallas as pl
from jax.experimental.pallas import tpu as pltpu
from jax.sharding import PartitionSpec as P

F32 = jnp.float32
BF16 = jnp.bfloat16
NT = (((1,), (1,)), ((), ()))


def pieces(x):
    hi = x.astype(BF16)
    rest = x - hi.astype(F32)
    mid = rest.astype(BF16)
    lo = (rest - mid.astype(F32)).astype(BF16)
    return hi, mid, lo


def times_transpose(rows, matrix):
    count = rows.shape[0]
    stacked = jnp.concatenate(pieces(rows), axis=0)
    out = lax.dot_general(stacked, matrix, NT, preferred_element_type=F32)
    return out[0:count] + out[count : 2 * count] + out[2 * count :]


def matvec_row(vector, matrix):
    hi, mid, lo = pieces(vector)
    width = vector.shape[1]
    row = lax.broadcasted_iota(jnp.int32, (8, width), 0)
    stacked = jnp.where(
        row == 0,
        hi.astype(F32),
        jnp.where(row == 1, mid.astype(F32), jnp.where(row == 2, lo.astype(F32), 0.0)),
    ).astype(BF16)
    out = lax.dot_general(stacked, matrix, NT, preferred_element_type=F32)
    return out[0:1] + out[1:2] + out[2:3]


def column_from_row(matrix, row):
    return jnp.sum(matrix * row, axis=1, keepdims=True)


def row_from_column(matrix_t, column):
    return jnp.sum(matrix_t * column, axis=0, keepdims=True)


BAND = 256


def transpose_into(dst, src):
    width = src.shape[0]
    for i in range(0, width, BAND):
        for j in range(0, width, BAND):
            dst[j : j + BAND, i : i + BAND] = src[i : i + BAND, j : j + BAND].T


def build_pairs(a_ref, g_ref, pair_ref, pair_t_ref):
    width = a_ref.shape[0]
    for start in range(0, width, BAND):
        rows = slice(start, start + BAND)
        a_rows = a_ref[rows, :].astype(F32)
        pair_ref[0, rows, :] = a_rows
        pair_ref[1, rows, :] = a_rows - jnp.dot(
            g_ref[rows, :], a_ref[...], preferred_element_type=F32
        )
    transpose_into(pair_t_ref.at[0], pair_ref.at[0])
    transpose_into(pair_t_ref.at[1], pair_ref.at[1])


def filter_kernel(
    flag_ref, prior_ref, w_ref, y_ref, a_ref, g_ref,
    even_ref, odd_ref, extra_ref, prev_ref, pair_ref, pair_t_ref,
):
    half = y_ref.shape[1]
    build_pairs(a_ref, g_ref, pair_ref, pair_t_ref)
    gain = g_ref[...]
    transition = a_ref[...]
    w_even, w_odd = w_ref[0], w_ref[1]
    y_even, y_odd = y_ref[0], y_ref[1]
    both = times_transpose(jnp.concatenate([y_even, y_odd], axis=0), gain)
    corr_even = w_even * both[:half]
    corr_odd = w_odd * both[half:]
    moved = times_transpose(corr_even, transition)
    extra_ref[...] = moved - w_odd * times_transpose(moved, gain) + corr_odd

    def pair_step(i, state):
        middle = column_from_row(pair_ref[flag_ref[2 * i]], state)
        updated = row_from_column(pair_t_ref[flag_ref[2 * i + 1]], middle)
        updated = updated + extra_ref[pl.ds(i, 1), :]
        odd_ref[pl.ds(i, 1), :] = updated
        return updated

    lax.fori_loop(0, half, pair_step, prior_ref[...])
    prev_ref[0:1, :] = prior_ref[...]
    prev_ref[1:half, :] = odd_ref[0 : half - 1, :]
    predicted = times_transpose(prev_ref[...], transition)
    even_ref[...] = predicted + w_even * times_transpose(y_even - predicted, gain)


def smooth_kernel(
    even_ref, odd_ref, a_ref, s_ref,
    s_even_ref, s_odd_ref, extra_ref, d_even_ref, s32_ref, s32_t_ref,
):
    half = even_ref.shape[0]
    width = s_ref.shape[0]
    for start in range(0, width, BAND):
        rows = slice(start, start + BAND)
        s32_ref[rows, :] = s_ref[rows, :].astype(F32)
    transpose_into(s32_t_ref, s32_ref)
    smoother = s_ref[...]
    transition = a_ref[...]
    both = jnp.concatenate([even_ref[...], odd_ref[...]], axis=0)
    d_both = both - times_transpose(times_transpose(both, transition), smoother)
    d_even_ref[...] = d_both[:half]
    d_odd = d_both[half:]
    pulled = times_transpose(d_even_ref[...], smoother)
    extra_ref[0 : half - 1, :] = pulled[1:half, :] + d_odd[0 : half - 1, :]
    last = odd_ref[half - 1 : half, :]
    s_odd_ref[half - 1 : half, :] = last

    def pair_step(j, state):
        r = half - 2 - j
        middle = column_from_row(s32_ref[...], state)
        value = row_from_column(s32_t_ref[...], middle) + extra_ref[pl.ds(r, 1), :]
        s_odd_ref[pl.ds(r, 1), :] = value
        return value

    lax.fori_loop(0, half - 1, pair_step, last)
    s_even_ref[...] = times_transpose(s_odd_ref[...], smoother) + d_even_ref[...]


VMEM_LIMIT = 60 * 1024 * 1024


def run_chain(weights, prior, transition, gain, smoother, observed):
    steps, width = observed.shape
    half = steps // 2
    vmem = pl.BlockSpec(memory_space=pltpu.VMEM)
    smem = pl.BlockSpec(memory_space=pltpu.SMEM)
    params = pltpu.CompilerParams(vmem_limit_bytes=VMEM_LIMIT)
    flags = weights.astype(jnp.int32)
    w_pair = weights.reshape(half, 2).T[:, :, None]
    y_pair = observed.reshape(half, 2, width).transpose(1, 0, 2)
    rows = jax.ShapeDtypeStruct((half, width), F32)
    square = pltpu.VMEM((width, width), F32)
    stacked = pltpu.VMEM((2, width, width), F32)
    f_even, f_odd = pl.pallas_call(
        filter_kernel,
        out_shape=(rows, rows),
        in_specs=[smem] + [vmem] * 5,
        out_specs=(vmem, vmem),
        scratch_shapes=[pltpu.VMEM((half, width), F32)] * 2 + [stacked, stacked],
        compiler_params=params,
    )(flags, prior, w_pair, y_pair, transition, gain)
    s_even, s_odd = pl.pallas_call(
        smooth_kernel,
        out_shape=(rows, rows),
        in_specs=[vmem] * 4,
        out_specs=(vmem, vmem),
        scratch_shapes=[pltpu.VMEM((half, width), F32)] * 2 + [square, square],
        compiler_params=params,
    )(f_even, f_odd, transition, smoother)
    return (f_even, f_odd), (s_even, s_odd)


def gather_kernel(count, block_ref, out_ref, local_sem, send_sems, recv_sems, swap_sems):
    me = lax.axis_index("tm")
    lane = lax.axis_index("state")
    core = lax.rem(lane, 2)
    sibling = lane + 1 - 2 * core
    half = count // 2
    share = half - 1
    mesh_id = pl.DeviceIdType.MESH
    barrier = pltpu.get_barrier_semaphore()
    for step in range(1, count):
        peer = lax.rem(me + step, count)
        pl.semaphore_signal(barrier, inc=1, device_id={"tm": peer}, device_id_type=mesh_id)
    pl.semaphore_signal(barrier, inc=1, device_id={"state": sibling}, device_id_type=mesh_id)
    pl.semaphore_wait(barrier, count)

    def fetch(step):
        peer = lax.rem(me + step, count)
        return pltpu.make_async_remote_copy(
            src_ref=block_ref,
            dst_ref=out_ref.at[step],
            send_sem=send_sems.at[step],
            recv_sem=recv_sems.at[step],
            device_id={"tm": peer},
            device_id_type=mesh_id,
        )

    own = pltpu.make_async_copy(block_ref, out_ref.at[0], local_sem)

    @pl.when(core == 0)
    def _():
        own.start()

    copies = [fetch(core * share + j + 1) for j in range(share)]
    for copy in copies:
        copy.start()
    last = fetch(count - 1)

    @pl.when(core == 1)
    def _():
        last.start()

    for copy in copies:
        copy.wait()

    @pl.when(core == 1)
    def _():
        last.wait()

    @pl.when(core == 0)
    def _():
        own.wait()

    mine = pl.ds(core * half, half)
    swap = pltpu.make_async_remote_copy(
        src_ref=out_ref.at[mine],
        dst_ref=out_ref.at[mine],
        send_sem=swap_sems.at[0],
        recv_sem=swap_sems.at[1],
        device_id={"state": sibling},
        device_id_type=mesh_id,
    )
    swap.start()
    swap.wait()


def gather_over_time(block):
    count = lax.axis_size("tm")
    vmem = pl.BlockSpec(memory_space=pltpu.VMEM)
    return pl.pallas_call(
        functools.partial(gather_kernel, count),
        out_shape=jax.ShapeDtypeStruct((count,) + block.shape, block.dtype),
        in_specs=[vmem],
        out_specs=vmem,
        scratch_shapes=[
            pltpu.SemaphoreType.DMA,
            pltpu.SemaphoreType.DMA((count,)),
            pltpu.SemaphoreType.DMA((count,)),
            pltpu.SemaphoreType.DMA((2,)),
        ],
        compiler_params=pltpu.CompilerParams(collective_id=0, has_side_effects=True),
    )(block)


def local(prior, transition, gain, smoother, observed, present):
    panel = smoother.shape[0]
    seg, width = observed.shape
    count = lax.axis_size("tm")
    me = lax.axis_index("tm")
    dense = seg * width // 128
    flags = jnp.zeros((8, 128), F32).at[0, :seg].set(present.astype(F32))
    block = jnp.concatenate([observed.reshape(dense, 128), flags], axis=0)
    slots = gather_over_time(block)
    order = lax.rem(me - jnp.arange(count) + count, count)
    slots = jnp.take(slots, order, axis=0)
    all_observed = slots[:, :dense, :].reshape(-1, width)
    weights = slots[:, dense, :seg].reshape(-1)
    smoother_full = lax.all_gather(smoother, "state", axis=0, tiled=True)
    (f_even, f_odd), (s_even, s_odd) = run_chain(
        weights, prior[None, :], transition, gain, smoother_full, all_observed
    )
    r0 = me * (seg // 2)
    c0 = lax.axis_index("state") * panel

    def block_of(even, odd):
        pick = lambda rows: lax.dynamic_slice(rows, (r0, c0), (seg // 2, panel))
        return jnp.stack([pick(even), pick(odd)], axis=1).reshape(seg, panel)

    return block_of(f_even, f_odd), block_of(s_even, s_odd)


def solution(mesh):
    placed = (P(), P(), P(), P("state", None), P("tm", None), P("tm"))
    return jax.shard_map(
        local,
        mesh=mesh,
        in_specs=placed,
        out_specs=(P("tm", "state"), P("tm", "state")),
        check_vma=False,
    )
```

```python
import functools

import jax
import jax.numpy as jnp
from jax import lax
from jax.experimental import pallas as pl
from jax.experimental.pallas import tpu as pltpu
from jax.sharding import PartitionSpec as P

F32 = jnp.float32
BF16 = jnp.bfloat16
NT = (((1,), (1,)), ((), ()))


def pieces(x):
    hi = x.astype(BF16)
    rest = x - hi.astype(F32)
    mid = rest.astype(BF16)
    lo = (rest - mid.astype(F32)).astype(BF16)
    return hi, mid, lo


def times_transpose(rows, matrix):
    count = rows.shape[0]
    stacked = jnp.concatenate(pieces(rows), axis=0)
    out = lax.dot_general(stacked, matrix, NT, preferred_element_type=F32)
    return out[0:count] + out[count : 2 * count] + out[2 * count :]


def matvec_row(vector, matrix):
    hi, mid, lo = pieces(vector)
    width = vector.shape[1]
    row = lax.broadcasted_iota(jnp.int32, (8, width), 0)
    stacked = jnp.where(
        row == 0,
        hi.astype(F32),
        jnp.where(row == 1, mid.astype(F32), jnp.where(row == 2, lo.astype(F32), 0.0)),
    ).astype(BF16)
    out = lax.dot_general(stacked, matrix, NT, preferred_element_type=F32)
    return out[0:1] + out[1:2] + out[2:3]


def column_from_row(matrix, row):
    return jnp.sum(matrix * row, axis=1, keepdims=True)


def row_from_column(matrix_t, column):
    return jnp.sum(matrix_t * column, axis=0, keepdims=True)


BAND = 256


def transpose_into(dst, src):
    width = src.shape[0]
    for i in range(0, width, BAND):
        for j in range(0, width, BAND):
            dst[j : j + BAND, i : i + BAND] = src[i : i + BAND, j : j + BAND].T


def build_pairs(a_ref, g_ref, pair_ref, pair_t_ref):
    width = a_ref.shape[0]
    for start in range(0, width, BAND):
        rows = slice(start, start + BAND)
        a_rows = a_ref[rows, :].astype(F32)
        pair_ref[0, rows, :] = a_rows
        pair_ref[1, rows, :] = a_rows - jnp.dot(
            g_ref[rows, :], a_ref[...], preferred_element_type=F32
        )
    transpose_into(pair_t_ref.at[0], pair_ref.at[0])
    transpose_into(pair_t_ref.at[1], pair_ref.at[1])


def filter_kernel(
    flag_ref, prior_ref, w_ref, y_ref, a_ref, g_ref,
    even_ref, odd_ref, extra_ref, prev_ref, pair_ref, pair_t_ref,
):
    half = y_ref.shape[1]
    build_pairs(a_ref, g_ref, pair_ref, pair_t_ref)
    gain = g_ref[...]
    transition = a_ref[...]
    w_even, w_odd = w_ref[0], w_ref[1]
    y_even, y_odd = y_ref[0], y_ref[1]
    both = times_transpose(jnp.concatenate([y_even, y_odd], axis=0), gain)
    corr_even = w_even * both[:half]
    corr_odd = w_odd * both[half:]
    moved = times_transpose(corr_even, transition)
    extra_ref[...] = moved - w_odd * times_transpose(moved, gain) + corr_odd

    def pair_step(i, state):
        middle = column_from_row(pair_ref[flag_ref[2 * i]], state)
        updated = row_from_column(pair_t_ref[flag_ref[2 * i + 1]], middle)
        updated = updated + extra_ref[pl.ds(i, 1), :]
        odd_ref[pl.ds(i, 1), :] = updated
        return updated

    lax.fori_loop(0, half, pair_step, prior_ref[...])
    prev_ref[0:1, :] = prior_ref[...]
    prev_ref[1:half, :] = odd_ref[0 : half - 1, :]
    predicted = times_transpose(prev_ref[...], transition)
    even_ref[...] = predicted + w_even * times_transpose(y_even - predicted, gain)


def smooth_kernel(
    even_ref, odd_ref, a_ref, s_ref,
    s_even_ref, s_odd_ref, u_ref, v_ref, t_ref, sq_ref, sq_t_ref,
):
    half = even_ref.shape[0]
    width = s_ref.shape[0]
    smoother = s_ref[...]
    transition = a_ref[...]
    for start in range(0, width, BAND):
        rows = slice(start, start + BAND)
        sq_ref[rows, :] = jnp.dot(s_ref[rows, :], smoother, preferred_element_type=F32)
    transpose_into(sq_t_ref, sq_ref)
    both = jnp.concatenate([even_ref[...], odd_ref[...]], axis=0)
    d_both = both - times_transpose(times_transpose(both, transition), smoother)
    d_even = d_both[:half]
    d_odd = d_both[half:]
    pulled = times_transpose(d_even, smoother)
    u_ref[0:1, :] = jnp.zeros((1, width), F32)
    u_ref[1:half, :] = pulled[1:half, :] + d_odd[0 : half - 1, :]
    twice = times_transpose(times_transpose(u_ref[...], smoother), smoother)
    v_ref[2:half, :] = twice[2:half, :] + u_ref[1 : half - 1, :]
    s_odd_ref[...] = jnp.zeros((half, width), F32)
    last = odd_ref[half - 1 : half, :]
    s_odd_ref[half - 1 : half, :] = last

    def quad_step(j, state):
        q = half - 1 - 2 * j
        middle = column_from_row(sq_ref[...], state)
        value = row_from_column(sq_t_ref[...], middle) + v_ref[pl.ds(q, 1), :]
        s_odd_ref[pl.ds(q - 2, 1), :] = value
        return value

    lax.fori_loop(0, half // 2 - 1, quad_step, last)
    odd_row = lax.broadcasted_iota(jnp.int32, (half, 1), 0) % 2 == 1
    first = times_transpose(s_odd_ref[...], smoother) + d_even
    s_even_ref[...] = jnp.where(odd_row, first, 0.0)
    t_ref[...] = times_transpose(s_even_ref[...], smoother)
    filled = t_ref[1:half, :] + d_odd[0 : half - 1, :]
    s_odd_ref[0 : half - 1, :] = jnp.where(odd_row[0 : half - 1], s_odd_ref[0 : half - 1, :], filled)
    third = times_transpose(s_odd_ref[...], smoother) + d_even
    s_even_ref[...] = jnp.where(odd_row, s_even_ref[...], third)


VMEM_LIMIT = 60 * 1024 * 1024


def run_chain(weights, prior, transition, gain, smoother, observed):
    steps, width = observed.shape
    half = steps // 2
    vmem = pl.BlockSpec(memory_space=pltpu.VMEM)
    smem = pl.BlockSpec(memory_space=pltpu.SMEM)
    params = pltpu.CompilerParams(vmem_limit_bytes=VMEM_LIMIT)
    flags = weights.astype(jnp.int32)
    w_pair = weights.reshape(half, 2).T[:, :, None]
    y_pair = observed.reshape(half, 2, width).transpose(1, 0, 2)
    rows = jax.ShapeDtypeStruct((half, width), F32)
    square = pltpu.VMEM((width, width), F32)
    stacked = pltpu.VMEM((2, width, width), F32)
    f_even, f_odd = pl.pallas_call(
        filter_kernel,
        out_shape=(rows, rows),
        in_specs=[smem] + [vmem] * 5,
        out_specs=(vmem, vmem),
        scratch_shapes=[pltpu.VMEM((half, width), F32)] * 2 + [stacked, stacked],
        compiler_params=params,
    )(flags, prior, w_pair, y_pair, transition, gain)
    s_even, s_odd = pl.pallas_call(
        smooth_kernel,
        out_shape=(rows, rows),
        in_specs=[vmem] * 4,
        out_specs=(vmem, vmem),
        scratch_shapes=[pltpu.VMEM((half, width), F32)] * 3 + [square, square],
        compiler_params=params,
    )(f_even, f_odd, transition, smoother)
    return (f_even, f_odd), (s_even, s_odd)


def gather_kernel(count, block_ref, out_ref, local_sem, send_sems, recv_sems, swap_sems):
    me = lax.axis_index("tm")
    lane = lax.axis_index("state")
    core = lax.rem(lane, 2)
    sibling = lane + 1 - 2 * core
    half = count // 2
    share = half - 1
    mesh_id = pl.DeviceIdType.MESH
    barrier = pltpu.get_barrier_semaphore()
    for step in range(1, count):
        peer = lax.rem(me + step, count)
        pl.semaphore_signal(barrier, inc=1, device_id={"tm": peer}, device_id_type=mesh_id)
    pl.semaphore_signal(barrier, inc=1, device_id={"state": sibling}, device_id_type=mesh_id)
    pl.semaphore_wait(barrier, count)

    def fetch(step):
        peer = lax.rem(me + step, count)
        return pltpu.make_async_remote_copy(
            src_ref=block_ref,
            dst_ref=out_ref.at[step],
            send_sem=send_sems.at[step],
            recv_sem=recv_sems.at[step],
            device_id={"tm": peer},
            device_id_type=mesh_id,
        )

    own = pltpu.make_async_copy(block_ref, out_ref.at[0], local_sem)

    @pl.when(core == 0)
    def _():
        own.start()

    copies = [fetch(core * share + j + 1) for j in range(share)]
    for copy in copies:
        copy.start()
    last = fetch(count - 1)

    @pl.when(core == 1)
    def _():
        last.start()

    for copy in copies:
        copy.wait()

    @pl.when(core == 1)
    def _():
        last.wait()

    @pl.when(core == 0)
    def _():
        own.wait()

    mine = pl.ds(core * half, half)
    swap = pltpu.make_async_remote_copy(
        src_ref=out_ref.at[mine],
        dst_ref=out_ref.at[mine],
        send_sem=swap_sems.at[0],
        recv_sem=swap_sems.at[1],
        device_id={"state": sibling},
        device_id_type=mesh_id,
    )
    swap.start()
    swap.wait()


def gather_over_time(block):
    count = lax.axis_size("tm")
    vmem = pl.BlockSpec(memory_space=pltpu.VMEM)
    return pl.pallas_call(
        functools.partial(gather_kernel, count),
        out_shape=jax.ShapeDtypeStruct((count,) + block.shape, block.dtype),
        in_specs=[vmem],
        out_specs=vmem,
        scratch_shapes=[
            pltpu.SemaphoreType.DMA,
            pltpu.SemaphoreType.DMA((count,)),
            pltpu.SemaphoreType.DMA((count,)),
            pltpu.SemaphoreType.DMA((2,)),
        ],
        compiler_params=pltpu.CompilerParams(collective_id=0, has_side_effects=True),
    )(block)


def local(prior, transition, gain, smoother, observed, present):
    panel = smoother.shape[0]
    seg, width = observed.shape
    count = lax.axis_size("tm")
    me = lax.axis_index("tm")
    dense = seg * width // 128
    flags = jnp.zeros((8, 128), F32).at[0, :seg].set(present.astype(F32))
    block = jnp.concatenate([observed.reshape(dense, 128), flags], axis=0)
    slots = gather_over_time(block)
    order = lax.rem(me - jnp.arange(count) + count, count)
    slots = jnp.take(slots, order, axis=0)
    all_observed = slots[:, :dense, :].reshape(-1, width)
    weights = slots[:, dense, :seg].reshape(-1)
    smoother_full = lax.all_gather(smoother, "state", axis=0, tiled=True)
    (f_even, f_odd), (s_even, s_odd) = run_chain(
        weights, prior[None, :], transition, gain, smoother_full, all_observed
    )
    r0 = me * (seg // 2)
    c0 = lax.axis_index("state") * panel

    def block_of(even, odd):
        pick = lambda rows: lax.dynamic_slice(rows, (r0, c0), (seg // 2, panel))
        return jnp.stack([pick(even), pick(odd)], axis=1).reshape(seg, panel)

    return block_of(f_even, f_odd), block_of(s_even, s_odd)


def solution(mesh):
    placed = (P(), P(), P(), P("state", None), P("tm", None), P("tm"))
    return jax.shard_map(
        local,
        mesh=mesh,
        in_specs=placed,
        out_specs=(P("tm", "state"), P("tm", "state")),
        check_vma=False,
    )
```

```python
import functools

import jax
import jax.numpy as jnp
from jax import lax
from jax.experimental import pallas as pl
from jax.experimental.pallas import tpu as pltpu
from jax.sharding import PartitionSpec as P

F32 = jnp.float32
BF16 = jnp.bfloat16
NT = (((1,), (1,)), ((), ()))


def pieces(x):
    hi = x.astype(BF16)
    rest = x - hi.astype(F32)
    mid = rest.astype(BF16)
    lo = (rest - mid.astype(F32)).astype(BF16)
    return hi, mid, lo


def times_transpose(rows, matrix):
    count = rows.shape[0]
    stacked = jnp.concatenate(pieces(rows), axis=0)
    out = lax.dot_general(stacked, matrix, NT, preferred_element_type=F32)
    return out[0:count] + out[count : 2 * count] + out[2 * count :]


def matvec_row(vector, matrix):
    hi, mid, lo = pieces(vector)
    width = vector.shape[1]
    row = lax.broadcasted_iota(jnp.int32, (8, width), 0)
    stacked = jnp.where(
        row == 0,
        hi.astype(F32),
        jnp.where(row == 1, mid.astype(F32), jnp.where(row == 2, lo.astype(F32), 0.0)),
    ).astype(BF16)
    out = lax.dot_general(stacked, matrix, NT, preferred_element_type=F32)
    return out[0:1] + out[1:2] + out[2:3]


def column_from_row(matrix, row):
    return jnp.sum(matrix * row, axis=1, keepdims=True)


def row_from_column(matrix_t, column):
    return jnp.sum(matrix_t * column, axis=0, keepdims=True)


BAND = 256


def transpose_into(dst, src):
    width = src.shape[0]
    for i in range(0, width, BAND):
        for j in range(0, width, BAND):
            dst[j : j + BAND, i : i + BAND] = src[i : i + BAND, j : j + BAND].T


def build_pairs(a_ref, g_ref, pair_ref, pair_t_ref):
    width = a_ref.shape[0]
    for start in range(0, width, BAND):
        rows = slice(start, start + BAND)
        a_rows = a_ref[rows, :].astype(F32)
        pair_ref[0, rows, :] = a_rows
        pair_ref[1, rows, :] = a_rows - jnp.dot(
            g_ref[rows, :], a_ref[...], preferred_element_type=F32
        )
    transpose_into(pair_t_ref.at[0], pair_ref.at[0])
    transpose_into(pair_t_ref.at[1], pair_ref.at[1])


def filter_kernel(
    flag_ref, prior_ref, w_ref, y_ref, a_ref, g_ref,
    even_ref, odd_ref, extra_ref, prev_ref, pair_ref, pair_t_ref,
):
    half = y_ref.shape[1]
    build_pairs(a_ref, g_ref, pair_ref, pair_t_ref)
    gain = g_ref[...]
    transition = a_ref[...]
    w_even, w_odd = w_ref[0], w_ref[1]
    y_even, y_odd = y_ref[0], y_ref[1]
    both = times_transpose(jnp.concatenate([y_even, y_odd], axis=0), gain)
    corr_even = w_even * both[:half]
    corr_odd = w_odd * both[half:]
    moved = times_transpose(corr_even, transition)
    extra_ref[...] = moved - w_odd * times_transpose(moved, gain) + corr_odd

    def pair_step(i, state):
        middle = column_from_row(pair_ref[flag_ref[2 * i]], state)
        updated = row_from_column(pair_t_ref[flag_ref[2 * i + 1]], middle)
        updated = updated + extra_ref[pl.ds(i, 1), :]
        odd_ref[pl.ds(i, 1), :] = updated
        return updated

    lax.fori_loop(0, half, pair_step, prior_ref[...])
    prev_ref[0:1, :] = prior_ref[...]
    prev_ref[1:half, :] = odd_ref[0 : half - 1, :]
    predicted = times_transpose(prev_ref[...], transition)
    even_ref[...] = predicted + w_even * times_transpose(y_even - predicted, gain)


def smooth_kernel(
    even_ref, odd_ref, a_ref, s_ref,
    s_even_ref, s_odd_ref, u_ref, v_ref, t_ref, sq_ref, sq_t_ref,
):
    half = even_ref.shape[0]
    width = s_ref.shape[0]
    smoother = s_ref[...]
    transition = a_ref[...]
    for start in range(0, width, BAND):
        rows = slice(start, start + BAND)
        sq_ref[rows, :] = jnp.dot(s_ref[rows, :], smoother, preferred_element_type=F32)
    transpose_into(sq_t_ref, sq_ref)
    both = jnp.concatenate([even_ref[...], odd_ref[...]], axis=0)
    d_both = both - times_transpose(times_transpose(both, transition), smoother)
    d_even = d_both[:half]
    d_odd = d_both[half:]
    pulled = times_transpose(d_even, smoother)
    u_ref[0:1, :] = jnp.zeros((1, width), F32)
    u_ref[1:half, :] = pulled[1:half, :] + d_odd[0 : half - 1, :]
    twice = times_transpose(times_transpose(u_ref[...], smoother), smoother)
    v_ref[2:half, :] = twice[2:half, :] + u_ref[1 : half - 1, :]
    s_odd_ref[...] = jnp.zeros((half, width), F32)
    last = odd_ref[half - 1 : half, :]
    s_odd_ref[half - 1 : half, :] = last

    def quad_step(j, state):
        q = half - 1 - 2 * j
        middle = column_from_row(sq_ref[...], state)
        value = row_from_column(sq_t_ref[...], middle) + v_ref[pl.ds(q, 1), :]
        s_odd_ref[pl.ds(q - 2, 1), :] = value
        return value

    lax.fori_loop(0, half // 2 - 1, quad_step, last)
    odd_row = lax.broadcasted_iota(jnp.int32, (half, 1), 0) % 2 == 1
    first = times_transpose(s_odd_ref[...], smoother) + d_even
    s_even_ref[...] = jnp.where(odd_row, first, 0.0)
    t_ref[...] = times_transpose(s_even_ref[...], smoother)
    filled = t_ref[1:half, :] + d_odd[0 : half - 1, :]
    s_odd_ref[0 : half - 1, :] = jnp.where(odd_row[0 : half - 1], s_odd_ref[0 : half - 1, :], filled)
    third = times_transpose(s_odd_ref[...], smoother) + d_even
    s_even_ref[...] = jnp.where(odd_row, s_even_ref[...], third)


VMEM_LIMIT = 60 * 1024 * 1024


def run_chain(weights, prior, transition, gain, smoother, observed):
    steps, width = observed.shape
    half = steps // 2
    vmem = pl.BlockSpec(memory_space=pltpu.VMEM)
    smem = pl.BlockSpec(memory_space=pltpu.SMEM)
    params = pltpu.CompilerParams(vmem_limit_bytes=VMEM_LIMIT)
    flags = weights.astype(jnp.int32)
    w_pair = weights.reshape(half, 2).T[:, :, None]
    y_pair = observed.reshape(half, 2, width).transpose(1, 0, 2)
    rows = jax.ShapeDtypeStruct((half, width), F32)
    square = pltpu.VMEM((width, width), F32)
    stacked = pltpu.VMEM((2, width, width), F32)
    f_even, f_odd = pl.pallas_call(
        filter_kernel,
        out_shape=(rows, rows),
        in_specs=[smem] + [vmem] * 5,
        out_specs=(vmem, vmem),
        scratch_shapes=[pltpu.VMEM((half, width), F32)] * 2 + [stacked, stacked],
        compiler_params=params,
    )(flags, prior, w_pair, y_pair, transition, gain)
    s_even, s_odd = pl.pallas_call(
        smooth_kernel,
        out_shape=(rows, rows),
        in_specs=[vmem] * 4,
        out_specs=(vmem, vmem),
        scratch_shapes=[pltpu.VMEM((half, width), F32)] * 3 + [square, square],
        compiler_params=params,
    )(f_even, f_odd, transition, smoother)
    return (f_even, f_odd), (s_even, s_odd)


def gather_kernel(count, block_ref, out_ref, local_sem, send_sems, recv_sems, swap_sems):
    me = lax.axis_index("tm")
    lane = lax.axis_index("state")
    core = lax.rem(lane, 2)
    sibling = lane + 1 - 2 * core
    half = count // 2
    share = half - 1
    mesh_id = pl.DeviceIdType.MESH
    barrier = pltpu.get_barrier_semaphore()
    for step in range(1, count):
        peer = lax.rem(me + step, count)
        pl.semaphore_signal(barrier, inc=1, device_id={"tm": peer}, device_id_type=mesh_id)
    pl.semaphore_signal(barrier, inc=1, device_id={"state": sibling}, device_id_type=mesh_id)
    pl.semaphore_wait(barrier, count)

    def fetch(step):
        peer = lax.rem(me + step, count)
        return pltpu.make_async_remote_copy(
            src_ref=block_ref,
            dst_ref=out_ref.at[step],
            send_sem=send_sems.at[step],
            recv_sem=recv_sems.at[step],
            device_id={"tm": peer},
            device_id_type=mesh_id,
        )

    own = pltpu.make_async_copy(block_ref, out_ref.at[0], local_sem)

    @pl.when(core == 0)
    def _():
        own.start()

    copies = [fetch(core * share + j + 1) for j in range(share)]
    for copy in copies:
        copy.start()
    last = fetch(count - 1)

    @pl.when(core == 1)
    def _():
        last.start()

    for copy in copies:
        copy.wait()

    @pl.when(core == 1)
    def _():
        last.wait()

    @pl.when(core == 0)
    def _():
        own.wait()

    mine = pl.ds(core * half, half)
    swap = pltpu.make_async_remote_copy(
        src_ref=out_ref.at[mine],
        dst_ref=out_ref.at[mine],
        send_sem=swap_sems.at[0],
        recv_sem=swap_sems.at[1],
        device_id={"state": sibling},
        device_id_type=mesh_id,
    )
    swap.start()
    swap.wait()


def gather_over_time(block):
    count = lax.axis_size("tm")
    vmem = pl.BlockSpec(memory_space=pltpu.VMEM)
    return pl.pallas_call(
        functools.partial(gather_kernel, count),
        out_shape=jax.ShapeDtypeStruct((count,) + block.shape, block.dtype),
        in_specs=[vmem],
        out_specs=vmem,
        scratch_shapes=[
            pltpu.SemaphoreType.DMA,
            pltpu.SemaphoreType.DMA((count,)),
            pltpu.SemaphoreType.DMA((count,)),
            pltpu.SemaphoreType.DMA((2,)),
        ],
        compiler_params=pltpu.CompilerParams(collective_id=0, has_side_effects=True),
    )(block)


def shifted(block, axis, count, distance):
    return lax.ppermute(block, axis, [(i, (i + distance) % count) for i in range(count)])


def gather_over_state(panel, tied):
    count = lax.axis_size("state")
    me = lax.axis_index("state")
    group = 1
    while group * group < count:
        group += 1
    if group * group != count:
        group = count
    first = jnp.stack([panel] + [shifted(panel, "state", count, d) for d in range(1, group)])
    first, tied = lax.optimization_barrier((first, tied))
    rounds = [first] + [
        shifted(first, "state", count, group * q) for q in range(1, count // group)
    ]
    stacked = jnp.concatenate(rounds, axis=0)
    order = lax.rem(me - jnp.arange(count) + count, count)
    stacked = jnp.take(stacked, order, axis=0)
    return stacked.reshape(count * panel.shape[0], panel.shape[1]), tied


def local(prior, transition, gain, smoother, observed, present):
    panel = smoother.shape[0]
    seg, width = observed.shape
    count = lax.axis_size("tm")
    me = lax.axis_index("tm")
    dense = seg * width // 128
    flags = jnp.zeros((8, 128), F32).at[0, :seg].set(present.astype(F32))
    block = jnp.concatenate([observed.reshape(dense, 128), flags], axis=0)
    slots = gather_over_time(block)
    order = lax.rem(me - jnp.arange(count) + count, count)
    slots = jnp.take(slots, order, axis=0)
    all_observed = slots[:, :dense, :].reshape(-1, width)
    weights = slots[:, dense, :seg].reshape(-1)
    smoother_full, all_observed = gather_over_state(smoother, all_observed)
    (f_even, f_odd), (s_even, s_odd) = run_chain(
        weights, prior[None, :], transition, gain, smoother_full, all_observed
    )
    r0 = me * (seg // 2)
    c0 = lax.axis_index("state") * panel

    def block_of(even, odd):
        pick = lambda rows: lax.dynamic_slice(rows, (r0, c0), (seg // 2, panel))
        return jnp.stack([pick(even), pick(odd)], axis=1).reshape(seg, panel)

    return block_of(f_even, f_odd), block_of(s_even, s_odd)


def solution(mesh):
    placed = (P(), P(), P(), P("state", None), P("tm", None), P("tm"))
    return jax.shard_map(
        local,
        mesh=mesh,
        in_specs=placed,
        out_specs=(P("tm", "state"), P("tm", "state")),
        check_vma=False,
    )
```

```python
import functools

import jax
import jax.numpy as jnp
from jax import lax
from jax.experimental import pallas as pl
from jax.experimental.pallas import tpu as pltpu
from jax.sharding import PartitionSpec as P

F32 = jnp.float32
BF16 = jnp.bfloat16
NT = (((1,), (1,)), ((), ()))


def pieces(x):
    hi = x.astype(BF16)
    rest = x - hi.astype(F32)
    mid = rest.astype(BF16)
    lo = (rest - mid.astype(F32)).astype(BF16)
    return hi, mid, lo


def times_transpose(rows, matrix):
    count = rows.shape[0]
    stacked = jnp.concatenate(pieces(rows), axis=0)
    out = lax.dot_general(stacked, matrix, NT, preferred_element_type=F32)
    return out[0:count] + out[count : 2 * count] + out[2 * count :]


def matvec_row(vector, matrix):
    hi, mid, lo = pieces(vector)
    width = vector.shape[1]
    row = lax.broadcasted_iota(jnp.int32, (8, width), 0)
    stacked = jnp.where(
        row == 0,
        hi.astype(F32),
        jnp.where(row == 1, mid.astype(F32), jnp.where(row == 2, lo.astype(F32), 0.0)),
    ).astype(BF16)
    out = lax.dot_general(stacked, matrix, NT, preferred_element_type=F32)
    return out[0:1] + out[1:2] + out[2:3]


def column_from_row(matrix, row):
    return jnp.sum(matrix * row, axis=1, keepdims=True)


def row_from_column(matrix_t, column):
    return jnp.sum(matrix_t * column, axis=0, keepdims=True)


BAND = 256


def transpose_into(dst, src):
    width = src.shape[0]
    for i in range(0, width, BAND):
        for j in range(0, width, BAND):
            dst[j : j + BAND, i : i + BAND] = src[i : i + BAND, j : j + BAND].T


def build_pairs(a_ref, g_ref, pair_ref, pair_t_ref):
    width = a_ref.shape[0]
    for start in range(0, width, BAND):
        rows = slice(start, start + BAND)
        a_rows = a_ref[rows, :].astype(F32)
        pair_ref[0, rows, :] = a_rows
        pair_ref[1, rows, :] = a_rows - jnp.dot(
            g_ref[rows, :], a_ref[...], preferred_element_type=F32
        )
    transpose_into(pair_t_ref.at[0], pair_ref.at[0])
    transpose_into(pair_t_ref.at[1], pair_ref.at[1])


def own_rows(even_ref, odd_ref, out_ref):
    per = out_ref.shape[0] // 2
    base = lax.axis_index("tm") * per
    for i in range(per):
        out_ref[2 * i : 2 * i + 1, :] = even_ref[pl.ds(base + i, 1), :]
        out_ref[2 * i + 1 : 2 * i + 2, :] = odd_ref[pl.ds(base + i, 1), :]


def filter_kernel(
    flag_ref, prior_ref, w_ref, y_ref, a_ref, g_ref,
    even_ref, odd_ref, own_ref, extra_ref, prev_ref, pair_ref, pair_t_ref,
):
    half = y_ref.shape[1]
    build_pairs(a_ref, g_ref, pair_ref, pair_t_ref)
    gain = g_ref[...]
    transition = a_ref[...]
    w_even, w_odd = w_ref[0], w_ref[1]
    y_even, y_odd = y_ref[0], y_ref[1]
    both = times_transpose(jnp.concatenate([y_even, y_odd], axis=0), gain)
    corr_even = w_even * both[:half]
    corr_odd = w_odd * both[half:]
    moved = times_transpose(corr_even, transition)
    extra_ref[...] = moved - w_odd * times_transpose(moved, gain) + corr_odd

    def pair_step(i, state):
        middle = column_from_row(pair_ref[flag_ref[2 * i]], state)
        updated = row_from_column(pair_t_ref[flag_ref[2 * i + 1]], middle)
        updated = updated + extra_ref[pl.ds(i, 1), :]
        odd_ref[pl.ds(i, 1), :] = updated
        return updated

    lax.fori_loop(0, half, pair_step, prior_ref[...])
    prev_ref[0:1, :] = prior_ref[...]
    prev_ref[1:half, :] = odd_ref[0 : half - 1, :]
    predicted = times_transpose(prev_ref[...], transition)
    even_ref[...] = predicted + w_even * times_transpose(y_even - predicted, gain)
    own_rows(even_ref, odd_ref, own_ref)


def smooth_kernel(
    even_ref, odd_ref, a_ref, s_ref,
    s_even_ref, s_odd_ref, own_ref, u_ref, v_ref, t_ref, sq_ref, sq_t_ref,
):
    half = even_ref.shape[0]
    width = s_ref.shape[0]
    smoother = s_ref[...]
    transition = a_ref[...]
    for start in range(0, width, BAND):
        rows = slice(start, start + BAND)
        sq_ref[rows, :] = jnp.dot(s_ref[rows, :], smoother, preferred_element_type=F32)
    transpose_into(sq_t_ref, sq_ref)
    both = jnp.concatenate([even_ref[...], odd_ref[...]], axis=0)
    d_both = both - times_transpose(times_transpose(both, transition), smoother)
    d_even = d_both[:half]
    d_odd = d_both[half:]
    pulled = times_transpose(d_even, smoother)
    u_ref[0:1, :] = jnp.zeros((1, width), F32)
    u_ref[1:half, :] = pulled[1:half, :] + d_odd[0 : half - 1, :]
    twice = times_transpose(times_transpose(u_ref[...], smoother), smoother)
    v_ref[2:half, :] = twice[2:half, :] + u_ref[1 : half - 1, :]
    s_odd_ref[...] = jnp.zeros((half, width), F32)
    last = odd_ref[half - 1 : half, :]
    s_odd_ref[half - 1 : half, :] = last

    def quad_step(j, state):
        q = half - 1 - 2 * j
        middle = column_from_row(sq_ref[...], state)
        value = row_from_column(sq_t_ref[...], middle) + v_ref[pl.ds(q, 1), :]
        s_odd_ref[pl.ds(q - 2, 1), :] = value
        return value

    lax.fori_loop(0, half // 2 - 1, quad_step, last)
    odd_row = lax.broadcasted_iota(jnp.int32, (half, 1), 0) % 2 == 1
    first = times_transpose(s_odd_ref[...], smoother) + d_even
    s_even_ref[...] = jnp.where(odd_row, first, 0.0)
    t_ref[...] = times_transpose(s_even_ref[...], smoother)
    filled = t_ref[1:half, :] + d_odd[0 : half - 1, :]
    s_odd_ref[0 : half - 1, :] = jnp.where(odd_row[0 : half - 1], s_odd_ref[0 : half - 1, :], filled)
    third = times_transpose(s_odd_ref[...], smoother) + d_even
    s_even_ref[...] = jnp.where(odd_row, s_even_ref[...], third)
    own_rows(s_even_ref, s_odd_ref, own_ref)


VMEM_LIMIT = 60 * 1024 * 1024


def run_chain(weights, prior, transition, gain, smoother, observed):
    steps, width = observed.shape
    half = steps // 2
    vmem = pl.BlockSpec(memory_space=pltpu.VMEM)
    smem = pl.BlockSpec(memory_space=pltpu.SMEM)
    params = pltpu.CompilerParams(vmem_limit_bytes=VMEM_LIMIT)
    flags = weights.astype(jnp.int32)
    w_pair = weights.reshape(half, 2).T[:, :, None]
    y_pair = observed.reshape(half, 2, width).transpose(1, 0, 2)
    rows = jax.ShapeDtypeStruct((half, width), F32)
    square = pltpu.VMEM((width, width), F32)
    stacked = pltpu.VMEM((2, width, width), F32)
    seg = steps // lax.axis_size("tm")
    own = jax.ShapeDtypeStruct((seg, width), F32)
    f_even, f_odd, f_own = pl.pallas_call(
        filter_kernel,
        out_shape=(rows, rows, own),
        in_specs=[smem] + [vmem] * 5,
        out_specs=(vmem, vmem, vmem),
        scratch_shapes=[pltpu.VMEM((half, width), F32)] * 2 + [stacked, stacked],
        compiler_params=params,
    )(flags, prior, w_pair, y_pair, transition, gain)
    _, _, s_own = pl.pallas_call(
        smooth_kernel,
        out_shape=(rows, rows, own),
        in_specs=[vmem] * 4,
        out_specs=(vmem, vmem, vmem),
        scratch_shapes=[pltpu.VMEM((half, width), F32)] * 3 + [square, square],
        compiler_params=params,
    )(f_even, f_odd, transition, smoother)
    return f_own, s_own


def gather_kernel(count, block_ref, out_ref, local_sem, send_sems, recv_sems, swap_sems):
    me = lax.axis_index("tm")
    lane = lax.axis_index("state")
    core = lax.rem(lane, 2)
    sibling = lane + 1 - 2 * core
    half = count // 2
    share = half - 1
    mesh_id = pl.DeviceIdType.MESH
    barrier = pltpu.get_barrier_semaphore()
    for step in range(1, count):
        peer = lax.rem(me + step, count)
        pl.semaphore_signal(barrier, inc=1, device_id={"tm": peer}, device_id_type=mesh_id)
    pl.semaphore_signal(barrier, inc=1, device_id={"state": sibling}, device_id_type=mesh_id)
    pl.semaphore_wait(barrier, count)

    def fetch(step):
        peer = lax.rem(me + step, count)
        return pltpu.make_async_remote_copy(
            src_ref=block_ref,
            dst_ref=out_ref.at[step],
            send_sem=send_sems.at[step],
            recv_sem=recv_sems.at[step],
            device_id={"tm": peer},
            device_id_type=mesh_id,
        )

    own = pltpu.make_async_copy(block_ref, out_ref.at[0], local_sem)

    @pl.when(core == 0)
    def _():
        own.start()

    copies = [fetch(core * share + j + 1) for j in range(share)]
    for copy in copies:
        copy.start()
    last = fetch(count - 1)

    @pl.when(core == 1)
    def _():
        last.start()

    for copy in copies:
        copy.wait()

    @pl.when(core == 1)
    def _():
        last.wait()

    @pl.when(core == 0)
    def _():
        own.wait()

    mine = pl.ds(core * half, half)
    swap = pltpu.make_async_remote_copy(
        src_ref=out_ref.at[mine],
        dst_ref=out_ref.at[mine],
        send_sem=swap_sems.at[0],
        recv_sem=swap_sems.at[1],
        device_id={"state": sibling},
        device_id_type=mesh_id,
    )
    swap.start()
    swap.wait()


def gather_over_time(block):
    count = lax.axis_size("tm")
    vmem = pl.BlockSpec(memory_space=pltpu.VMEM)
    return pl.pallas_call(
        functools.partial(gather_kernel, count),
        out_shape=jax.ShapeDtypeStruct((count,) + block.shape, block.dtype),
        in_specs=[vmem],
        out_specs=vmem,
        scratch_shapes=[
            pltpu.SemaphoreType.DMA,
            pltpu.SemaphoreType.DMA((count,)),
            pltpu.SemaphoreType.DMA((count,)),
            pltpu.SemaphoreType.DMA((2,)),
        ],
        compiler_params=pltpu.CompilerParams(collective_id=0, has_side_effects=True),
    )(block)


def local(prior, transition, gain, smoother, observed, present):
    panel = smoother.shape[0]
    seg, width = observed.shape
    count = lax.axis_size("tm")
    me = lax.axis_index("tm")
    dense = seg * width // 128
    flags = jnp.zeros((8, 128), F32).at[0, :seg].set(present.astype(F32))
    block = jnp.concatenate([observed.reshape(dense, 128), flags], axis=0)
    slots = gather_over_time(block)
    order = lax.rem(me - jnp.arange(count) + count, count)
    slots = jnp.take(slots, order, axis=0)
    all_observed = slots[:, :dense, :].reshape(-1, width)
    weights = slots[:, dense, :seg].reshape(-1)
    smoother_full = lax.all_gather(smoother, "state", axis=0, tiled=True)
    f_own, s_own = run_chain(
        weights, prior[None, :], transition, gain, smoother_full, all_observed
    )
    c0 = lax.axis_index("state") * panel
    block_of = lambda rows: lax.dynamic_slice_in_dim(rows, c0, panel, 1)
    return block_of(f_own), block_of(s_own)


def solution(mesh):
    placed = (P(), P(), P(), P("state", None), P("tm", None), P("tm"))
    return jax.shard_map(
        local,
        mesh=mesh,
        in_specs=placed,
        out_specs=(P("tm", "state"), P("tm", "state")),
        check_vma=False,
    )
```

```python
import functools

import jax
import jax.numpy as jnp
from jax import lax
from jax.experimental import pallas as pl
from jax.experimental.pallas import tpu as pltpu
from jax.sharding import PartitionSpec as P

F32 = jnp.float32
BF16 = jnp.bfloat16
NT = (((1,), (1,)), ((), ()))


def pieces(x):
    hi = x.astype(BF16)
    rest = x - hi.astype(F32)
    mid = rest.astype(BF16)
    lo = (rest - mid.astype(F32)).astype(BF16)
    return hi, mid, lo


def times_transpose(rows, matrix):
    count = rows.shape[0]
    stacked = jnp.concatenate(pieces(rows), axis=0)
    out = lax.dot_general(stacked, matrix, NT, preferred_element_type=F32)
    return out[0:count] + out[count : 2 * count] + out[2 * count :]


def matvec_row(vector, matrix):
    hi, mid, lo = pieces(vector)
    width = vector.shape[1]
    row = lax.broadcasted_iota(jnp.int32, (8, width), 0)
    stacked = jnp.where(
        row == 0,
        hi.astype(F32),
        jnp.where(row == 1, mid.astype(F32), jnp.where(row == 2, lo.astype(F32), 0.0)),
    ).astype(BF16)
    out = lax.dot_general(stacked, matrix, NT, preferred_element_type=F32)
    return out[0:1] + out[1:2] + out[2:3]


def column_from_row(matrix, row):
    return jnp.sum(matrix * row, axis=1, keepdims=True)


def row_from_column(matrix_t, column):
    return jnp.sum(matrix_t * column, axis=0, keepdims=True)


BAND = 256


def transpose_into(dst, src):
    width = src.shape[0]
    for i in range(0, width, BAND):
        for j in range(0, width, BAND):
            dst[j : j + BAND, i : i + BAND] = src[i : i + BAND, j : j + BAND].T


def build_pairs(a_ref, g_ref, pair_ref, pair_t_ref):
    width = a_ref.shape[0]
    for start in range(0, width, BAND):
        rows = slice(start, start + BAND)
        a_rows = a_ref[rows, :].astype(F32)
        pair_ref[0, rows, :] = a_rows
        pair_ref[1, rows, :] = a_rows - jnp.dot(
            g_ref[rows, :], a_ref[...], preferred_element_type=F32
        )
    transpose_into(pair_t_ref.at[0], pair_ref.at[0])
    transpose_into(pair_t_ref.at[1], pair_ref.at[1])


def own_rows(even_ref, odd_ref, out_ref):
    per = out_ref.shape[0] // 2
    panel = out_ref.shape[1]
    width = even_ref.shape[1]
    base = lax.axis_index("tm") * per
    lane = lax.axis_index("state")
    rows = []
    for i in range(per):
        rows.append(even_ref[pl.ds(base + i, 1), :])
        rows.append(odd_ref[pl.ds(base + i, 1), :])
    block = jnp.concatenate(rows, axis=0)
    picked = block[:, 0:panel]
    for j in range(1, width // panel):
        picked = jnp.where(lane == j, block[:, j * panel : (j + 1) * panel], picked)
    out_ref[...] = picked


def filter_kernel(
    flag_ref, prior_ref, w_ref, y_ref, a_ref, g_ref,
    even_ref, odd_ref, own_ref, extra_ref, prev_ref, pair_ref, pair_t_ref,
):
    half = y_ref.shape[1]
    build_pairs(a_ref, g_ref, pair_ref, pair_t_ref)
    gain = g_ref[...]
    transition = a_ref[...]
    w_even, w_odd = w_ref[0], w_ref[1]
    y_even, y_odd = y_ref[0], y_ref[1]
    both = times_transpose(jnp.concatenate([y_even, y_odd], axis=0), gain)
    corr_even = w_even * both[:half]
    corr_odd = w_odd * both[half:]
    moved = times_transpose(corr_even, transition)
    extra_ref[...] = moved - w_odd * times_transpose(moved, gain) + corr_odd

    def pair_step(i, state):
        middle = column_from_row(pair_ref[flag_ref[2 * i]], state)
        updated = row_from_column(pair_t_ref[flag_ref[2 * i + 1]], middle)
        updated = updated + extra_ref[pl.ds(i, 1), :]
        odd_ref[pl.ds(i, 1), :] = updated
        return updated

    lax.fori_loop(0, half, pair_step, prior_ref[...])
    prev_ref[0:1, :] = prior_ref[...]
    prev_ref[1:half, :] = odd_ref[0 : half - 1, :]
    predicted = times_transpose(prev_ref[...], transition)
    even_ref[...] = predicted + w_even * times_transpose(y_even - predicted, gain)
    own_rows(even_ref, odd_ref, own_ref)


def smooth_kernel(
    even_ref, odd_ref, a_ref, s_ref,
    s_even_ref, s_odd_ref, own_ref, u_ref, v_ref, t_ref, sq_ref, sq_t_ref,
):
    half = even_ref.shape[0]
    width = s_ref.shape[0]
    smoother = s_ref[...]
    transition = a_ref[...]
    for start in range(0, width, BAND):
        rows = slice(start, start + BAND)
        sq_ref[rows, :] = jnp.dot(s_ref[rows, :], smoother, preferred_element_type=F32)
    transpose_into(sq_t_ref, sq_ref)
    both = jnp.concatenate([even_ref[...], odd_ref[...]], axis=0)
    d_both = both - times_transpose(times_transpose(both, transition), smoother)
    d_even = d_both[:half]
    d_odd = d_both[half:]
    pulled = times_transpose(d_even, smoother)
    u_ref[0:1, :] = jnp.zeros((1, width), F32)
    u_ref[1:half, :] = pulled[1:half, :] + d_odd[0 : half - 1, :]
    twice = times_transpose(times_transpose(u_ref[...], smoother), smoother)
    v_ref[2:half, :] = twice[2:half, :] + u_ref[1 : half - 1, :]
    s_odd_ref[...] = jnp.zeros((half, width), F32)
    last = odd_ref[half - 1 : half, :]
    s_odd_ref[half - 1 : half, :] = last

    def quad_step(j, state):
        q = half - 1 - 2 * j
        middle = column_from_row(sq_ref[...], state)
        value = row_from_column(sq_t_ref[...], middle) + v_ref[pl.ds(q, 1), :]
        s_odd_ref[pl.ds(q - 2, 1), :] = value
        return value

    lax.fori_loop(0, half // 2 - 1, quad_step, last)
    odd_row = lax.broadcasted_iota(jnp.int32, (half, 1), 0) % 2 == 1
    first = times_transpose(s_odd_ref[...], smoother) + d_even
    s_even_ref[...] = jnp.where(odd_row, first, 0.0)
    t_ref[...] = times_transpose(s_even_ref[...], smoother)
    filled = t_ref[1:half, :] + d_odd[0 : half - 1, :]
    s_odd_ref[0 : half - 1, :] = jnp.where(odd_row[0 : half - 1], s_odd_ref[0 : half - 1, :], filled)
    third = times_transpose(s_odd_ref[...], smoother) + d_even
    s_even_ref[...] = jnp.where(odd_row, s_even_ref[...], third)
    own_rows(s_even_ref, s_odd_ref, own_ref)


VMEM_LIMIT = 60 * 1024 * 1024


def run_chain(weights, prior, transition, gain, smoother, observed):
    steps, width = observed.shape
    half = steps // 2
    vmem = pl.BlockSpec(memory_space=pltpu.VMEM)
    smem = pl.BlockSpec(memory_space=pltpu.SMEM)
    params = pltpu.CompilerParams(vmem_limit_bytes=VMEM_LIMIT)
    flags = weights.astype(jnp.int32)
    w_pair = weights.reshape(half, 2).T[:, :, None]
    y_pair = observed.reshape(half, 2, width).transpose(1, 0, 2)
    rows = jax.ShapeDtypeStruct((half, width), F32)
    square = pltpu.VMEM((width, width), F32)
    stacked = pltpu.VMEM((2, width, width), F32)
    seg = steps // lax.axis_size("tm")
    own = jax.ShapeDtypeStruct((seg, width // lax.axis_size("state")), F32)
    f_even, f_odd, f_own = pl.pallas_call(
        filter_kernel,
        out_shape=(rows, rows, own),
        in_specs=[smem] + [vmem] * 5,
        out_specs=(vmem, vmem, vmem),
        scratch_shapes=[pltpu.VMEM((half, width), F32)] * 2 + [stacked, stacked],
        compiler_params=params,
    )(flags, prior, w_pair, y_pair, transition, gain)
    _, _, s_own = pl.pallas_call(
        smooth_kernel,
        out_shape=(rows, rows, own),
        in_specs=[vmem] * 4,
        out_specs=(vmem, vmem, vmem),
        scratch_shapes=[pltpu.VMEM((half, width), F32)] * 3 + [square, square],
        compiler_params=params,
    )(f_even, f_odd, transition, smoother)
    return f_own, s_own


def gather_kernel(count, block_ref, out_ref, local_sem, send_sems, recv_sems, swap_sems):
    me = lax.axis_index("tm")
    lane = lax.axis_index("state")
    core = lax.rem(lane, 2)
    sibling = lane + 1 - 2 * core
    half = count // 2
    share = half - 1
    mesh_id = pl.DeviceIdType.MESH
    barrier = pltpu.get_barrier_semaphore()
    for step in range(1, count):
        peer = lax.rem(me + step, count)
        pl.semaphore_signal(barrier, inc=1, device_id={"tm": peer}, device_id_type=mesh_id)
    pl.semaphore_signal(barrier, inc=1, device_id={"state": sibling}, device_id_type=mesh_id)
    pl.semaphore_wait(barrier, count)

    def fetch(step):
        peer = lax.rem(me + step, count)
        return pltpu.make_async_remote_copy(
            src_ref=block_ref,
            dst_ref=out_ref.at[step],
            send_sem=send_sems.at[step],
            recv_sem=recv_sems.at[step],
            device_id={"tm": peer},
            device_id_type=mesh_id,
        )

    own = pltpu.make_async_copy(block_ref, out_ref.at[0], local_sem)

    @pl.when(core == 0)
    def _():
        own.start()

    copies = [fetch(core * share + j + 1) for j in range(share)]
    for copy in copies:
        copy.start()
    last = fetch(count - 1)

    @pl.when(core == 1)
    def _():
        last.start()

    for copy in copies:
        copy.wait()

    @pl.when(core == 1)
    def _():
        last.wait()

    @pl.when(core == 0)
    def _():
        own.wait()

    mine = pl.ds(core * half, half)
    swap = pltpu.make_async_remote_copy(
        src_ref=out_ref.at[mine],
        dst_ref=out_ref.at[mine],
        send_sem=swap_sems.at[0],
        recv_sem=swap_sems.at[1],
        device_id={"state": sibling},
        device_id_type=mesh_id,
    )
    swap.start()
    swap.wait()


def gather_over_time(block):
    count = lax.axis_size("tm")
    vmem = pl.BlockSpec(memory_space=pltpu.VMEM)
    return pl.pallas_call(
        functools.partial(gather_kernel, count),
        out_shape=jax.ShapeDtypeStruct((count,) + block.shape, block.dtype),
        in_specs=[vmem],
        out_specs=vmem,
        scratch_shapes=[
            pltpu.SemaphoreType.DMA,
            pltpu.SemaphoreType.DMA((count,)),
            pltpu.SemaphoreType.DMA((count,)),
            pltpu.SemaphoreType.DMA((2,)),
        ],
        compiler_params=pltpu.CompilerParams(collective_id=0, has_side_effects=True),
    )(block)


def local(prior, transition, gain, smoother, observed, present):
    panel = smoother.shape[0]
    seg, width = observed.shape
    count = lax.axis_size("tm")
    me = lax.axis_index("tm")
    dense = seg * width // 128
    flags = jnp.zeros((8, 128), F32).at[0, :seg].set(present.astype(F32))
    block = jnp.concatenate([observed.reshape(dense, 128), flags], axis=0)
    slots = gather_over_time(block)
    order = lax.rem(me - jnp.arange(count) + count, count)
    slots = jnp.take(slots, order, axis=0)
    all_observed = slots[:, :dense, :].reshape(-1, width)
    weights = slots[:, dense, :seg].reshape(-1)
    smoother_full = lax.all_gather(smoother, "state", axis=0, tiled=True)
    f_own, s_own = run_chain(
        weights, prior[None, :], transition, gain, smoother_full, all_observed
    )
    return f_own, s_own


def solution(mesh):
    placed = (P(), P(), P(), P("state", None), P("tm", None), P("tm"))
    return jax.shard_map(
        local,
        mesh=mesh,
        in_specs=placed,
        out_specs=(P("tm", "state"), P("tm", "state")),
        check_vma=False,
    )
```

```python
import functools

import jax
import jax.numpy as jnp
from jax import lax
from jax.experimental import pallas as pl
from jax.experimental.pallas import tpu as pltpu
from jax.sharding import PartitionSpec as P

F32 = jnp.float32
BF16 = jnp.bfloat16
NT = (((1,), (1,)), ((), ()))


def pieces(x):
    hi = x.astype(BF16)
    rest = x - hi.astype(F32)
    mid = rest.astype(BF16)
    lo = (rest - mid.astype(F32)).astype(BF16)
    return hi, mid, lo


def times_transpose(rows, matrix):
    count = rows.shape[0]
    stacked = jnp.concatenate(pieces(rows), axis=0)
    out = lax.dot_general(stacked, matrix, NT, preferred_element_type=F32)
    return out[0:count] + out[count : 2 * count] + out[2 * count :]


def matvec_row(vector, matrix):
    hi, mid, lo = pieces(vector)
    width = vector.shape[1]
    row = lax.broadcasted_iota(jnp.int32, (8, width), 0)
    stacked = jnp.where(
        row == 0,
        hi.astype(F32),
        jnp.where(row == 1, mid.astype(F32), jnp.where(row == 2, lo.astype(F32), 0.0)),
    ).astype(BF16)
    out = lax.dot_general(stacked, matrix, NT, preferred_element_type=F32)
    return out[0:1] + out[1:2] + out[2:3]


def column_from_row(matrix, row):
    return jnp.sum(matrix * row, axis=1, keepdims=True)


def row_from_column(matrix_t, column):
    return jnp.sum(matrix_t * column, axis=0, keepdims=True)


BAND = 256


def transpose_into(dst, src):
    width = src.shape[0]
    for i in range(0, width, BAND):
        for j in range(0, width, BAND):
            dst[j : j + BAND, i : i + BAND] = src[i : i + BAND, j : j + BAND].T


def build_pairs(a_ref, g_ref, pair_ref, pair_t_ref):
    width = a_ref.shape[0]
    for start in range(0, width, BAND):
        rows = slice(start, start + BAND)
        a_rows = a_ref[rows, :].astype(F32)
        pair_ref[0, rows, :] = a_rows
        pair_ref[1, rows, :] = a_rows - jnp.dot(
            g_ref[rows, :], a_ref[...], preferred_element_type=F32
        )
    transpose_into(pair_t_ref.at[0], pair_ref.at[0])
    transpose_into(pair_t_ref.at[1], pair_ref.at[1])


def own_rows(even_ref, odd_ref, out_ref):
    per = out_ref.shape[0] // 2
    panel = out_ref.shape[1]
    width = even_ref.shape[1]
    base = lax.axis_index("tm") * per
    lane = lax.axis_index("state")
    rows = []
    for i in range(per):
        rows.append(even_ref[pl.ds(base + i, 1), :])
        rows.append(odd_ref[pl.ds(base + i, 1), :])
    block = jnp.concatenate(rows, axis=0)
    picked = block[:, 0:panel]
    for j in range(1, width // panel):
        picked = jnp.where(lane == j, block[:, j * panel : (j + 1) * panel], picked)
    out_ref[...] = picked


def filter_kernel(
    flag_ref, prior_ref, w_ref, y_ref, a_ref, g_ref,
    even_ref, odd_ref, own_ref, extra_ref, prev_ref, pair_ref, pair_t_ref,
):
    half = y_ref.shape[1]
    build_pairs(a_ref, g_ref, pair_ref, pair_t_ref)
    gain = g_ref[...]
    transition = a_ref[...]
    w_even, w_odd = w_ref[0], w_ref[1]
    y_even, y_odd = y_ref[0], y_ref[1]
    both = times_transpose(jnp.concatenate([y_even, y_odd], axis=0), gain)
    corr_even = w_even * both[:half]
    corr_odd = w_odd * both[half:]
    moved = times_transpose(corr_even, transition)
    extra_ref[...] = moved - w_odd * times_transpose(moved, gain) + corr_odd

    def pair_step(i, state):
        middle = column_from_row(pair_ref[flag_ref[2 * i]], state)
        updated = row_from_column(pair_t_ref[flag_ref[2 * i + 1]], middle)
        updated = updated + extra_ref[pl.ds(i, 1), :]
        odd_ref[pl.ds(i, 1), :] = updated
        return updated

    lax.fori_loop(0, half, pair_step, prior_ref[...])
    prev_ref[0:1, :] = prior_ref[...]
    prev_ref[1:half, :] = odd_ref[0 : half - 1, :]
    predicted = times_transpose(prev_ref[...], transition)
    even_ref[...] = predicted + w_even * times_transpose(y_even - predicted, gain)
    own_rows(even_ref, odd_ref, own_ref)


def smooth_kernel(
    even_ref, odd_ref, a_ref, s_ref,
    s_even_ref, s_odd_ref, own_ref, u_ref, v_ref, t_ref, sq_ref, sq_t_ref,
):
    half = even_ref.shape[0]
    width = s_ref.shape[0]
    smoother = s_ref[...]
    transition = a_ref[...]
    for start in range(0, width, BAND):
        rows = slice(start, start + BAND)
        sq_ref[rows, :] = jnp.dot(s_ref[rows, :], smoother, preferred_element_type=F32)
    transpose_into(sq_t_ref, sq_ref)
    both = jnp.concatenate([even_ref[...], odd_ref[...]], axis=0)
    d_both = both - times_transpose(times_transpose(both, transition), smoother)
    d_even = d_both[:half]
    d_odd = d_both[half:]
    pulled = times_transpose(d_even, smoother)
    u_ref[0:1, :] = jnp.zeros((1, width), F32)
    u_ref[1:half, :] = pulled[1:half, :] + d_odd[0 : half - 1, :]
    twice = times_transpose(times_transpose(u_ref[...], smoother), smoother)
    v_ref[2:half, :] = twice[2:half, :] + u_ref[1 : half - 1, :]
    s_odd_ref[...] = jnp.zeros((half, width), F32)
    last = odd_ref[half - 1 : half, :]
    s_odd_ref[half - 1 : half, :] = last

    def quad_step(j, state):
        q = half - 1 - 2 * j
        middle = column_from_row(sq_ref[...], state)
        value = row_from_column(sq_t_ref[...], middle) + v_ref[pl.ds(q, 1), :]
        s_odd_ref[pl.ds(q - 2, 1), :] = value
        return value

    lax.fori_loop(0, half // 2 - 1, quad_step, last)
    odd_row = lax.broadcasted_iota(jnp.int32, (half, 1), 0) % 2 == 1
    first = times_transpose(s_odd_ref[...], smoother) + d_even
    s_even_ref[...] = jnp.where(odd_row, first, 0.0)
    t_ref[...] = times_transpose(s_even_ref[...], smoother)
    filled = t_ref[1:half, :] + d_odd[0 : half - 1, :]
    s_odd_ref[0 : half - 1, :] = jnp.where(odd_row[0 : half - 1], s_odd_ref[0 : half - 1, :], filled)
    third = times_transpose(s_odd_ref[...], smoother) + d_even
    s_even_ref[...] = jnp.where(odd_row, s_even_ref[...], third)
    own_rows(s_even_ref, s_odd_ref, own_ref)


VMEM_LIMIT = 60 * 1024 * 1024


def run_chain(weights, prior, transition, gain, smoother, observed):
    steps, width = observed.shape
    half = steps // 2
    vmem = pl.BlockSpec(memory_space=pltpu.VMEM)
    smem = pl.BlockSpec(memory_space=pltpu.SMEM)
    params = pltpu.CompilerParams(vmem_limit_bytes=VMEM_LIMIT)
    flags = weights.astype(jnp.int32)
    w_pair = weights.reshape(half, 2).T[:, :, None]
    y_pair = observed.reshape(half, 2, width).transpose(1, 0, 2)
    rows = jax.ShapeDtypeStruct((half, width), F32)
    square = pltpu.VMEM((width, width), F32)
    stacked = pltpu.VMEM((2, width, width), F32)
    seg = steps // lax.axis_size("tm")
    own = jax.ShapeDtypeStruct((seg, width // lax.axis_size("state")), F32)
    f_even, f_odd, f_own = pl.pallas_call(
        filter_kernel,
        out_shape=(rows, rows, own),
        in_specs=[smem] + [vmem] * 5,
        out_specs=(vmem, vmem, vmem),
        scratch_shapes=[pltpu.VMEM((half, width), F32)] * 2 + [stacked, stacked],
        compiler_params=params,
    )(flags, prior, w_pair, y_pair, transition, gain)
    _, _, s_own = pl.pallas_call(
        smooth_kernel,
        out_shape=(rows, rows, own),
        in_specs=[vmem] * 4,
        out_specs=(vmem, vmem, vmem),
        scratch_shapes=[pltpu.VMEM((half, width), F32)] * 3 + [square, square],
        compiler_params=params,
    )(f_even, f_odd, transition, smoother)
    return f_own, s_own


def gather_kernel(count, block_ref, out_ref, local_sem, send_sems, recv_sems, swap_sems):
    me = lax.axis_index("tm")
    lane = lax.axis_index("state")
    core = lax.rem(lane, 2)
    sibling = lane + 1 - 2 * core
    half = count // 2
    share = half - 1
    mesh_id = pl.DeviceIdType.MESH
    barrier = pltpu.get_barrier_semaphore()
    for step in range(1, count):
        peer = lax.rem(me + step, count)
        pl.semaphore_signal(barrier, inc=1, device_id={"tm": peer}, device_id_type=mesh_id)
    pl.semaphore_signal(barrier, inc=1, device_id={"state": sibling}, device_id_type=mesh_id)
    pl.semaphore_wait(barrier, count)

    def fetch(step):
        peer = lax.rem(me + step, count)
        return pltpu.make_async_remote_copy(
            src_ref=block_ref,
            dst_ref=out_ref.at[step],
            send_sem=send_sems.at[step],
            recv_sem=recv_sems.at[step],
            device_id={"tm": peer},
            device_id_type=mesh_id,
        )

    own = pltpu.make_async_copy(block_ref, out_ref.at[0], local_sem)

    @pl.when(core == 0)
    def _():
        own.start()

    copies = [fetch(core * share + j + 1) for j in range(share)]
    for copy in copies:
        copy.start()
    last = fetch(count - 1)

    @pl.when(core == 1)
    def _():
        last.start()

    for copy in copies:
        copy.wait()

    @pl.when(core == 1)
    def _():
        last.wait()

    @pl.when(core == 0)
    def _():
        own.wait()

    mine = pl.ds(core * half, half)
    swap = pltpu.make_async_remote_copy(
        src_ref=out_ref.at[mine],
        dst_ref=out_ref.at[mine],
        send_sem=swap_sems.at[0],
        recv_sem=swap_sems.at[1],
        device_id={"state": sibling},
        device_id_type=mesh_id,
    )
    swap.start()
    swap.wait()


def gather_over_time(block):
    count = lax.axis_size("tm")
    vmem = pl.BlockSpec(memory_space=pltpu.VMEM)
    return pl.pallas_call(
        functools.partial(gather_kernel, count),
        out_shape=jax.ShapeDtypeStruct((count,) + block.shape, block.dtype),
        in_specs=[vmem],
        out_specs=vmem,
        scratch_shapes=[
            pltpu.SemaphoreType.DMA,
            pltpu.SemaphoreType.DMA((count,)),
            pltpu.SemaphoreType.DMA((count,)),
            pltpu.SemaphoreType.DMA((2,)),
        ],
        compiler_params=pltpu.CompilerParams(collective_id=0, has_side_effects=True),
    )(block)


def local(prior, transition, gain, smoother, observed, present):
    panel = smoother.shape[0]
    seg, width = observed.shape
    count = lax.axis_size("tm")
    me = lax.axis_index("tm")
    dense = seg * width // 128
    flags = jnp.zeros((8, 128), F32).at[0, :seg].set(present.astype(F32))
    block = jnp.concatenate([observed.reshape(dense, 128), flags], axis=0)
    slots = gather_over_time(block)
    smoother, slots = lax.optimization_barrier((smoother, slots))
    order = lax.rem(me - jnp.arange(count) + count, count)
    slots = jnp.take(slots, order, axis=0)
    all_observed = slots[:, :dense, :].reshape(-1, width)
    weights = slots[:, dense, :seg].reshape(-1)
    smoother_full = lax.all_gather(smoother, "state", axis=0, tiled=True)
    f_own, s_own = run_chain(
        weights, prior[None, :], transition, gain, smoother_full, all_observed
    )
    return f_own, s_own


def solution(mesh):
    placed = (P(), P(), P(), P("state", None), P("tm", None), P("tm"))
    return jax.shard_map(
        local,
        mesh=mesh,
        in_specs=placed,
        out_specs=(P("tm", "state"), P("tm", "state")),
        check_vma=False,
    )
```

```python
import functools

import jax
import jax.numpy as jnp
from jax import lax
from jax.experimental import pallas as pl
from jax.experimental.pallas import tpu as pltpu
from jax.sharding import PartitionSpec as P

F32 = jnp.float32
BF16 = jnp.bfloat16
NT = (((1,), (1,)), ((), ()))


def pieces(x):
    hi = x.astype(BF16)
    rest = x - hi.astype(F32)
    mid = rest.astype(BF16)
    lo = (rest - mid.astype(F32)).astype(BF16)
    return hi, mid, lo


def times_transpose(rows, matrix):
    count = rows.shape[0]
    stacked = jnp.concatenate(pieces(rows), axis=0)
    out = lax.dot_general(stacked, matrix, NT, preferred_element_type=F32)
    return out[0:count] + out[count : 2 * count] + out[2 * count :]


def matvec_row(vector, matrix):
    hi, mid, lo = pieces(vector)
    width = vector.shape[1]
    row = lax.broadcasted_iota(jnp.int32, (8, width), 0)
    stacked = jnp.where(
        row == 0,
        hi.astype(F32),
        jnp.where(row == 1, mid.astype(F32), jnp.where(row == 2, lo.astype(F32), 0.0)),
    ).astype(BF16)
    out = lax.dot_general(stacked, matrix, NT, preferred_element_type=F32)
    return out[0:1] + out[1:2] + out[2:3]


def column_from_row(matrix, row):
    return jnp.sum(matrix * row, axis=1, keepdims=True)


def row_from_column(matrix_t, column):
    return jnp.sum(matrix_t * column, axis=0, keepdims=True)


BAND = 256


def transpose_into(dst, src):
    width = src.shape[0]
    for i in range(0, width, BAND):
        for j in range(0, width, BAND):
            dst[j : j + BAND, i : i + BAND] = src[i : i + BAND, j : j + BAND].T


def build_pairs(a_ref, g_ref, pair_ref, pair_t_ref):
    width = a_ref.shape[0]
    for start in range(0, width, BAND):
        rows = slice(start, start + BAND)
        a_rows = a_ref[rows, :].astype(F32)
        pair_ref[0, rows, :] = a_rows
        pair_ref[1, rows, :] = a_rows - jnp.dot(
            g_ref[rows, :], a_ref[...], preferred_element_type=F32
        )
    transpose_into(pair_t_ref.at[0], pair_ref.at[0])
    transpose_into(pair_t_ref.at[1], pair_ref.at[1])


def own_rows(even_ref, odd_ref, out_ref):
    per = out_ref.shape[0] // 2
    panel = out_ref.shape[1]
    width = even_ref.shape[1]
    base = lax.axis_index("tm") * per
    lane = lax.axis_index("state")
    rows = []
    for i in range(per):
        rows.append(even_ref[pl.ds(base + i, 1), :])
        rows.append(odd_ref[pl.ds(base + i, 1), :])
    block = jnp.concatenate(rows, axis=0)
    picked = block[:, 0:panel]
    for j in range(1, width // panel):
        picked = jnp.where(lane == j, block[:, j * panel : (j + 1) * panel], picked)
    out_ref[...] = picked


def filter_kernel(
    flag_ref, prior_ref, w_ref, y_ref, a_ref, g_ref,
    even_ref, odd_ref, own_ref, extra_ref, prev_ref, pair_ref, pair_t_ref,
):
    half = y_ref.shape[1]
    build_pairs(a_ref, g_ref, pair_ref, pair_t_ref)
    gain = g_ref[...]
    transition = a_ref[...]
    w_even, w_odd = w_ref[0], w_ref[1]
    y_even, y_odd = y_ref[0], y_ref[1]
    both = times_transpose(jnp.concatenate([y_even, y_odd], axis=0), gain)
    corr_even = w_even * both[:half]
    corr_odd = w_odd * both[half:]
    moved = times_transpose(corr_even, transition)
    extra_ref[...] = moved - w_odd * times_transpose(moved, gain) + corr_odd

    def pair_step(i, state):
        middle = column_from_row(pair_ref[flag_ref[2 * i]], state)
        updated = row_from_column(pair_t_ref[flag_ref[2 * i + 1]], middle)
        updated = updated + extra_ref[pl.ds(i, 1), :]
        odd_ref[pl.ds(i, 1), :] = updated
        return updated

    lax.fori_loop(0, half, pair_step, prior_ref[...])
    prev_ref[0:1, :] = prior_ref[...]
    prev_ref[1:half, :] = odd_ref[0 : half - 1, :]
    predicted = times_transpose(prev_ref[...], transition)
    even_ref[...] = predicted + w_even * times_transpose(y_even - predicted, gain)
    own_rows(even_ref, odd_ref, own_ref)


def smooth_kernel(
    even_ref, odd_ref, a_ref, s_ref,
    s_even_ref, s_odd_ref, own_ref, u_ref, v_ref, t_ref, sq_ref, sq_t_ref,
):
    half = even_ref.shape[0]
    width = s_ref.shape[0]
    smoother = s_ref[...]
    transition = a_ref[...]
    for start in range(0, width, BAND):
        rows = slice(start, start + BAND)
        sq_ref[rows, :] = jnp.dot(s_ref[rows, :], smoother, preferred_element_type=F32)
    transpose_into(sq_t_ref, sq_ref)
    both = jnp.concatenate([even_ref[...], odd_ref[...]], axis=0)
    d_both = both - times_transpose(times_transpose(both, transition), smoother)
    d_even = d_both[:half]
    d_odd = d_both[half:]
    pulled = times_transpose(d_even, smoother)
    u_ref[0:1, :] = jnp.zeros((1, width), F32)
    u_ref[1:half, :] = pulled[1:half, :] + d_odd[0 : half - 1, :]
    twice = times_transpose(times_transpose(u_ref[...], smoother), smoother)
    v_ref[2:half, :] = twice[2:half, :] + u_ref[1 : half - 1, :]
    s_odd_ref[...] = jnp.zeros((half, width), F32)
    last = odd_ref[half - 1 : half, :]
    s_odd_ref[half - 1 : half, :] = last

    def quad_step(j, state):
        q = half - 1 - 2 * j
        middle = column_from_row(sq_ref[...], state)
        value = row_from_column(sq_t_ref[...], middle) + v_ref[pl.ds(q, 1), :]
        s_odd_ref[pl.ds(q - 2, 1), :] = value
        return value

    lax.fori_loop(0, half // 2 - 1, quad_step, last)
    odd_row = lax.broadcasted_iota(jnp.int32, (half, 1), 0) % 2 == 1
    first = times_transpose(s_odd_ref[...], smoother) + d_even
    s_even_ref[...] = jnp.where(odd_row, first, 0.0)
    t_ref[...] = times_transpose(s_even_ref[...], smoother)
    filled = t_ref[1:half, :] + d_odd[0 : half - 1, :]
    s_odd_ref[0 : half - 1, :] = jnp.where(odd_row[0 : half - 1], s_odd_ref[0 : half - 1, :], filled)
    third = times_transpose(s_odd_ref[...], smoother) + d_even
    s_even_ref[...] = jnp.where(odd_row, s_even_ref[...], third)
    own_rows(s_even_ref, s_odd_ref, own_ref)


VMEM_LIMIT = 60 * 1024 * 1024


def run_chain(weights, prior, transition, gain, smoother, observed):
    steps, width = observed.shape
    half = steps // 2
    vmem = pl.BlockSpec(memory_space=pltpu.VMEM)
    smem = pl.BlockSpec(memory_space=pltpu.SMEM)
    params = pltpu.CompilerParams(vmem_limit_bytes=VMEM_LIMIT)
    flags = weights.astype(jnp.int32)
    w_pair = weights.reshape(half, 2).T[:, :, None]
    y_pair = observed.reshape(half, 2, width).transpose(1, 0, 2)
    rows = jax.ShapeDtypeStruct((half, width), F32)
    square = pltpu.VMEM((width, width), F32)
    stacked = pltpu.VMEM((2, width, width), F32)
    seg = steps // lax.axis_size("tm")
    own = jax.ShapeDtypeStruct((seg, width // lax.axis_size("state")), F32)
    f_even, f_odd, f_own = pl.pallas_call(
        filter_kernel,
        out_shape=(rows, rows, own),
        in_specs=[smem] + [vmem] * 5,
        out_specs=(vmem, vmem, vmem),
        scratch_shapes=[pltpu.VMEM((half, width), F32)] * 2 + [stacked, stacked],
        compiler_params=params,
    )(flags, prior, w_pair, y_pair, transition, gain)
    _, _, s_own = pl.pallas_call(
        smooth_kernel,
        out_shape=(rows, rows, own),
        in_specs=[vmem] * 4,
        out_specs=(vmem, vmem, vmem),
        scratch_shapes=[pltpu.VMEM((half, width), F32)] * 3 + [square, square],
        compiler_params=params,
    )(f_even, f_odd, transition, smoother)
    return f_own, s_own


def gather_kernel(count, block_ref, out_ref, local_sem, send_sems, recv_sems, swap_sems):
    me = lax.axis_index("tm")
    lane = lax.axis_index("state")
    core = lax.rem(lane, 2)
    sibling = lane + 1 - 2 * core
    half = count // 2
    share = half - 1
    mesh_id = pl.DeviceIdType.MESH

    def fetch(step):
        peer = lax.rem(me + step, count)
        return pltpu.make_async_remote_copy(
            src_ref=block_ref,
            dst_ref=out_ref.at[step],
            send_sem=send_sems.at[step],
            recv_sem=recv_sems.at[step],
            device_id={"tm": peer},
            device_id_type=mesh_id,
        )

    own = pltpu.make_async_copy(block_ref, out_ref.at[0], local_sem)

    @pl.when(core == 0)
    def _():
        own.start()

    copies = [fetch(core * share + j + 1) for j in range(share)]
    for copy in copies:
        copy.start()
    last = fetch(count - 1)

    @pl.when(core == 1)
    def _():
        last.start()

    for copy in copies:
        copy.wait()

    @pl.when(core == 1)
    def _():
        last.wait()

    @pl.when(core == 0)
    def _():
        own.wait()

    mine = pl.ds(core * half, half)
    swap = pltpu.make_async_remote_copy(
        src_ref=out_ref.at[mine],
        dst_ref=out_ref.at[mine],
        send_sem=swap_sems.at[0],
        recv_sem=swap_sems.at[1],
        device_id={"state": sibling},
        device_id_type=mesh_id,
    )
    swap.start()
    swap.wait()


def gather_over_time(block):
    count = lax.axis_size("tm")
    vmem = pl.BlockSpec(memory_space=pltpu.VMEM)
    return pl.pallas_call(
        functools.partial(gather_kernel, count),
        out_shape=jax.ShapeDtypeStruct((count,) + block.shape, block.dtype),
        in_specs=[vmem],
        out_specs=vmem,
        scratch_shapes=[
            pltpu.SemaphoreType.DMA,
            pltpu.SemaphoreType.DMA((count,)),
            pltpu.SemaphoreType.DMA((count,)),
            pltpu.SemaphoreType.DMA((2,)),
        ],
        compiler_params=pltpu.CompilerParams(has_side_effects=True),
    )(block)


def local(prior, transition, gain, smoother, observed, present):
    panel = smoother.shape[0]
    seg, width = observed.shape
    count = lax.axis_size("tm")
    me = lax.axis_index("tm")
    dense = seg * width // 128
    flags = jnp.zeros((8, 128), F32).at[0, :seg].set(present.astype(F32))
    block = jnp.concatenate([observed.reshape(dense, 128), flags], axis=0)
    slots = gather_over_time(block)
    order = lax.rem(me - jnp.arange(count) + count, count)
    slots = jnp.take(slots, order, axis=0)
    all_observed = slots[:, :dense, :].reshape(-1, width)
    weights = slots[:, dense, :seg].reshape(-1)
    smoother_full = lax.all_gather(smoother, "state", axis=0, tiled=True)
    f_own, s_own = run_chain(
        weights, prior[None, :], transition, gain, smoother_full, all_observed
    )
    return f_own, s_own


def solution(mesh):
    placed = (P(), P(), P(), P("state", None), P("tm", None), P("tm"))
    return jax.shard_map(
        local,
        mesh=mesh,
        in_specs=placed,
        out_specs=(P("tm", "state"), P("tm", "state")),
        check_vma=False,
    )
```

```python
import functools

import jax
import jax.numpy as jnp
from jax import lax
from jax.experimental import pallas as pl
from jax.experimental.pallas import tpu as pltpu
from jax.sharding import PartitionSpec as P

F32 = jnp.float32
BF16 = jnp.bfloat16
NT = (((1,), (1,)), ((), ()))


def pieces(x):
    hi = x.astype(BF16)
    rest = x - hi.astype(F32)
    mid = rest.astype(BF16)
    lo = (rest - mid.astype(F32)).astype(BF16)
    return hi, mid, lo


def times_transpose(rows, matrix):
    count = rows.shape[0]
    stacked = jnp.concatenate(pieces(rows), axis=0)
    out = lax.dot_general(stacked, matrix, NT, preferred_element_type=F32)
    return out[0:count] + out[count : 2 * count] + out[2 * count :]


def matvec_row(vector, matrix):
    hi, mid, lo = pieces(vector)
    width = vector.shape[1]
    row = lax.broadcasted_iota(jnp.int32, (8, width), 0)
    stacked = jnp.where(
        row == 0,
        hi.astype(F32),
        jnp.where(row == 1, mid.astype(F32), jnp.where(row == 2, lo.astype(F32), 0.0)),
    ).astype(BF16)
    out = lax.dot_general(stacked, matrix, NT, preferred_element_type=F32)
    return out[0:1] + out[1:2] + out[2:3]


def column_from_row(matrix, row):
    return jnp.sum(matrix * row, axis=1, keepdims=True)


def row_from_column(matrix_t, column):
    return jnp.sum(matrix_t * column, axis=0, keepdims=True)


BAND = 256


def transpose_into(dst, src):
    width = src.shape[0]
    for i in range(0, width, BAND):
        for j in range(0, width, BAND):
            dst[j : j + BAND, i : i + BAND] = src[i : i + BAND, j : j + BAND].T


def build_pairs(a_ref, g_ref, pair_ref, pair_t_ref):
    width = a_ref.shape[0]
    for start in range(0, width, BAND):
        rows = slice(start, start + BAND)
        a_rows = a_ref[rows, :].astype(F32)
        pair_ref[0, rows, :] = a_rows
        pair_ref[1, rows, :] = a_rows - jnp.dot(
            g_ref[rows, :], a_ref[...], preferred_element_type=F32
        )
    transpose_into(pair_t_ref.at[0], pair_ref.at[0])
    transpose_into(pair_t_ref.at[1], pair_ref.at[1])


def own_rows(even_ref, odd_ref, out_ref):
    per = out_ref.shape[0] // 2
    panel = out_ref.shape[1]
    width = even_ref.shape[1]
    base = lax.axis_index("tm") * per
    lane = lax.axis_index("state")
    rows = []
    for i in range(per):
        rows.append(even_ref[pl.ds(base + i, 1), :])
        rows.append(odd_ref[pl.ds(base + i, 1), :])
    block = jnp.concatenate(rows, axis=0)
    picked = block[:, 0:panel]
    for j in range(1, width // panel):
        picked = jnp.where(lane == j, block[:, j * panel : (j + 1) * panel], picked)
    out_ref[...] = picked


def filter_kernel(
    flag_ref, prior_ref, w_ref, y_ref, a_ref, g_ref,
    even_ref, odd_ref, own_ref, extra_ref, prev_ref, pair_ref, pair_t_ref,
):
    half = y_ref.shape[1]
    build_pairs(a_ref, g_ref, pair_ref, pair_t_ref)
    gain = g_ref[...]
    transition = a_ref[...]
    w_even, w_odd = w_ref[0], w_ref[1]
    y_even, y_odd = y_ref[0], y_ref[1]
    both = times_transpose(jnp.concatenate([y_even, y_odd], axis=0), gain)
    corr_even = w_even * both[:half]
    corr_odd = w_odd * both[half:]
    moved = times_transpose(corr_even, transition)
    extra_ref[...] = moved - w_odd * times_transpose(moved, gain) + corr_odd

    def pair_step(i, state):
        middle = column_from_row(pair_ref[flag_ref[2 * i]], state)
        updated = row_from_column(pair_t_ref[flag_ref[2 * i + 1]], middle)
        updated = updated + extra_ref[pl.ds(i, 1), :]
        odd_ref[pl.ds(i, 1), :] = updated
        return updated

    lax.fori_loop(0, half, pair_step, prior_ref[...])
    prev_ref[0:1, :] = prior_ref[...]
    prev_ref[1:half, :] = odd_ref[0 : half - 1, :]
    predicted = times_transpose(prev_ref[...], transition)
    even_ref[...] = predicted + w_even * times_transpose(y_even - predicted, gain)
    own_rows(even_ref, odd_ref, own_ref)


def smooth_kernel(
    even_ref, odd_ref, a_ref, s_ref,
    s_even_ref, s_odd_ref, own_ref, u_ref, v_ref, t_ref, sq_ref, sq_t_ref,
):
    half = even_ref.shape[0]
    width = s_ref.shape[0]
    smoother = s_ref[...]
    transition = a_ref[...]
    for start in range(0, width, BAND):
        rows = slice(start, start + BAND)
        sq_ref[rows, :] = jnp.dot(s_ref[rows, :], smoother, preferred_element_type=F32)
    transpose_into(sq_t_ref, sq_ref)
    both = jnp.concatenate([even_ref[...], odd_ref[...]], axis=0)
    d_both = both - times_transpose(times_transpose(both, transition), smoother)
    d_even = d_both[:half]
    d_odd = d_both[half:]
    pulled = times_transpose(d_even, smoother)
    u_ref[0:1, :] = jnp.zeros((1, width), F32)
    u_ref[1:half, :] = pulled[1:half, :] + d_odd[0 : half - 1, :]
    twice = times_transpose(times_transpose(u_ref[...], smoother), smoother)
    v_ref[2:half, :] = twice[2:half, :] + u_ref[1 : half - 1, :]
    s_odd_ref[...] = jnp.zeros((half, width), F32)
    last = odd_ref[half - 1 : half, :]
    s_odd_ref[half - 1 : half, :] = last

    def quad_step(j, state):
        q = half - 1 - 2 * j
        middle = column_from_row(sq_ref[...], state)
        value = row_from_column(sq_t_ref[...], middle) + v_ref[pl.ds(q, 1), :]
        s_odd_ref[pl.ds(q - 2, 1), :] = value
        return value

    lax.fori_loop(0, half // 2 - 1, quad_step, last)
    odd_row = lax.broadcasted_iota(jnp.int32, (half, 1), 0) % 2 == 1
    first = times_transpose(s_odd_ref[...], smoother) + d_even
    s_even_ref[...] = jnp.where(odd_row, first, 0.0)
    t_ref[...] = times_transpose(s_even_ref[...], smoother)
    filled = t_ref[1:half, :] + d_odd[0 : half - 1, :]
    s_odd_ref[0 : half - 1, :] = jnp.where(odd_row[0 : half - 1], s_odd_ref[0 : half - 1, :], filled)
    third = times_transpose(s_odd_ref[...], smoother) + d_even
    s_even_ref[...] = jnp.where(odd_row, s_even_ref[...], third)
    own_rows(s_even_ref, s_odd_ref, own_ref)


VMEM_LIMIT = 60 * 1024 * 1024


def run_chain(weights, prior, transition, gain, smoother, observed):
    steps, width = observed.shape
    half = steps // 2
    vmem = pl.BlockSpec(memory_space=pltpu.VMEM)
    smem = pl.BlockSpec(memory_space=pltpu.SMEM)
    params = pltpu.CompilerParams(vmem_limit_bytes=VMEM_LIMIT)
    flags = weights.astype(jnp.int32)
    w_pair = weights.reshape(half, 2).T[:, :, None]
    y_pair = observed.reshape(half, 2, width).transpose(1, 0, 2)
    rows = jax.ShapeDtypeStruct((half, width), F32)
    square = pltpu.VMEM((width, width), F32)
    stacked = pltpu.VMEM((2, width, width), F32)
    seg = steps // lax.axis_size("tm")
    own = jax.ShapeDtypeStruct((seg, width // lax.axis_size("state")), F32)
    f_even, f_odd, f_own = pl.pallas_call(
        filter_kernel,
        out_shape=(rows, rows, own),
        in_specs=[smem] + [vmem] * 5,
        out_specs=(vmem, vmem, vmem),
        scratch_shapes=[pltpu.VMEM((half, width), F32)] * 2 + [stacked, stacked],
        compiler_params=params,
    )(flags, prior, w_pair, y_pair, transition, gain)
    _, _, s_own = pl.pallas_call(
        smooth_kernel,
        out_shape=(rows, rows, own),
        in_specs=[vmem] * 4,
        out_specs=(vmem, vmem, vmem),
        scratch_shapes=[pltpu.VMEM((half, width), F32)] * 3 + [square, square],
        compiler_params=params,
    )(f_even, f_odd, transition, smoother)
    return f_own, s_own


def gather_kernel(count, block_ref, out_ref, local_sem, send_sems, recv_sems, swap_sems):
    me = lax.axis_index("tm")
    lane = lax.axis_index("state")
    core = lax.rem(lane, 2)
    sibling = lane + 1 - 2 * core
    half = count // 2
    share = half - 1
    mesh_id = pl.DeviceIdType.MESH
    barrier = pltpu.get_barrier_semaphore()

    def greet(step):
        peer = lax.rem(me - step + count, count)
        pl.semaphore_signal(barrier, inc=1, device_id={"tm": peer}, device_id_type=mesh_id)

    for j in range(half - 1):
        greet(core * (half - 1) + j + 1)

    @pl.when(core == 1)
    def _():
        greet(count - 1)

    pl.semaphore_signal(barrier, inc=1, device_id={"state": sibling}, device_id_type=mesh_id)
    pl.semaphore_wait(barrier, half + core)

    def fetch(step):
        peer = lax.rem(me + step, count)
        return pltpu.make_async_remote_copy(
            src_ref=block_ref,
            dst_ref=out_ref.at[step],
            send_sem=send_sems.at[step],
            recv_sem=recv_sems.at[step],
            device_id={"tm": peer},
            device_id_type=mesh_id,
        )

    own = pltpu.make_async_copy(block_ref, out_ref.at[0], local_sem)

    @pl.when(core == 0)
    def _():
        own.start()

    copies = [fetch(core * share + j + 1) for j in range(share)]
    for copy in copies:
        copy.start()
    last = fetch(count - 1)

    @pl.when(core == 1)
    def _():
        last.start()

    for copy in copies:
        copy.wait()

    @pl.when(core == 1)
    def _():
        last.wait()

    @pl.when(core == 0)
    def _():
        own.wait()

    mine = pl.ds(core * half, half)
    swap = pltpu.make_async_remote_copy(
        src_ref=out_ref.at[mine],
        dst_ref=out_ref.at[mine],
        send_sem=swap_sems.at[0],
        recv_sem=swap_sems.at[1],
        device_id={"state": sibling},
        device_id_type=mesh_id,
    )
    swap.start()
    swap.wait()


def gather_over_time(block):
    count = lax.axis_size("tm")
    vmem = pl.BlockSpec(memory_space=pltpu.VMEM)
    return pl.pallas_call(
        functools.partial(gather_kernel, count),
        out_shape=jax.ShapeDtypeStruct((count,) + block.shape, block.dtype),
        in_specs=[vmem],
        out_specs=vmem,
        scratch_shapes=[
            pltpu.SemaphoreType.DMA,
            pltpu.SemaphoreType.DMA((count,)),
            pltpu.SemaphoreType.DMA((count,)),
            pltpu.SemaphoreType.DMA((2,)),
        ],
        compiler_params=pltpu.CompilerParams(collective_id=0, has_side_effects=True),
    )(block)


def local(prior, transition, gain, smoother, observed, present):
    panel = smoother.shape[0]
    seg, width = observed.shape
    count = lax.axis_size("tm")
    me = lax.axis_index("tm")
    dense = seg * width // 128
    flags = jnp.zeros((8, 128), F32).at[0, :seg].set(present.astype(F32))
    block = jnp.concatenate([observed.reshape(dense, 128), flags], axis=0)
    slots = gather_over_time(block)
    smoother, slots = lax.optimization_barrier((smoother, slots))
    order = lax.rem(me - jnp.arange(count) + count, count)
    slots = jnp.take(slots, order, axis=0)
    all_observed = slots[:, :dense, :].reshape(-1, width)
    weights = slots[:, dense, :seg].reshape(-1)
    smoother_full = lax.all_gather(smoother, "state", axis=0, tiled=True)
    f_own, s_own = run_chain(
        weights, prior[None, :], transition, gain, smoother_full, all_observed
    )
    return f_own, s_own


def solution(mesh):
    placed = (P(), P(), P(), P("state", None), P("tm", None), P("tm"))
    return jax.shard_map(
        local,
        mesh=mesh,
        in_specs=placed,
        out_specs=(P("tm", "state"), P("tm", "state")),
        check_vma=False,
    )
```

```python
import functools

import jax
import jax.numpy as jnp
from jax import lax
from jax.experimental import pallas as pl
from jax.experimental.pallas import tpu as pltpu
from jax.sharding import PartitionSpec as P

F32 = jnp.float32
BF16 = jnp.bfloat16
NT = (((1,), (1,)), ((), ()))


def pieces(x):
    hi = x.astype(BF16)
    rest = x - hi.astype(F32)
    mid = rest.astype(BF16)
    lo = (rest - mid.astype(F32)).astype(BF16)
    return hi, mid, lo


def times_transpose(rows, matrix):
    count = rows.shape[0]
    stacked = jnp.concatenate(pieces(rows), axis=0)
    out = lax.dot_general(stacked, matrix, NT, preferred_element_type=F32)
    return out[0:count] + out[count : 2 * count] + out[2 * count :]


def matvec_row(vector, matrix):
    hi, mid, lo = pieces(vector)
    width = vector.shape[1]
    row = lax.broadcasted_iota(jnp.int32, (8, width), 0)
    stacked = jnp.where(
        row == 0,
        hi.astype(F32),
        jnp.where(row == 1, mid.astype(F32), jnp.where(row == 2, lo.astype(F32), 0.0)),
    ).astype(BF16)
    out = lax.dot_general(stacked, matrix, NT, preferred_element_type=F32)
    return out[0:1] + out[1:2] + out[2:3]


def column_from_row(matrix, row):
    return jnp.sum(matrix * row, axis=1, keepdims=True)


def row_from_column(matrix_t, column):
    return jnp.sum(matrix_t * column, axis=0, keepdims=True)


BAND = 256


def transpose_into(dst, src):
    width = src.shape[0]
    for i in range(0, width, BAND):
        for j in range(0, width, BAND):
            dst[j : j + BAND, i : i + BAND] = src[i : i + BAND, j : j + BAND].T


def build_pairs(a_ref, g_ref, pair_ref, pair_t_ref):
    width = a_ref.shape[0]
    for start in range(0, width, BAND):
        rows = slice(start, start + BAND)
        a_rows = a_ref[rows, :].astype(F32)
        pair_ref[0, rows, :] = a_rows
        pair_ref[1, rows, :] = a_rows - jnp.dot(
            g_ref[rows, :], a_ref[...], preferred_element_type=F32
        )
    transpose_into(pair_t_ref.at[0], pair_ref.at[0])
    transpose_into(pair_t_ref.at[1], pair_ref.at[1])


def own_rows(even_ref, odd_ref, out_ref):
    per = out_ref.shape[0] // 2
    panel = out_ref.shape[1]
    width = even_ref.shape[1]
    base = lax.axis_index("tm") * per
    lane = lax.axis_index("state")
    rows = []
    for i in range(per):
        rows.append(even_ref[pl.ds(base + i, 1), :])
        rows.append(odd_ref[pl.ds(base + i, 1), :])
    block = jnp.concatenate(rows, axis=0)
    picked = block[:, 0:panel]
    for j in range(1, width // panel):
        picked = jnp.where(lane == j, block[:, j * panel : (j + 1) * panel], picked)
    out_ref[...] = picked


def filter_kernel(
    flag_ref, prior_ref, w_ref, y_ref, a_ref, g_ref,
    even_ref, odd_ref, own_ref, extra_ref, prev_ref, pair_ref, pair_t_ref,
):
    half = y_ref.shape[1]
    build_pairs(a_ref, g_ref, pair_ref, pair_t_ref)
    gain = g_ref[...]
    transition = a_ref[...]
    w_even, w_odd = w_ref[0], w_ref[1]
    y_even, y_odd = y_ref[0], y_ref[1]
    both = times_transpose(jnp.concatenate([y_even, y_odd], axis=0), gain)
    corr_even = w_even * both[:half]
    corr_odd = w_odd * both[half:]
    moved = times_transpose(corr_even, transition)
    extra_ref[...] = moved - w_odd * times_transpose(moved, gain) + corr_odd

    def pair_step(i, state):
        middle = column_from_row(pair_ref[flag_ref[2 * i]], state)
        updated = row_from_column(pair_t_ref[flag_ref[2 * i + 1]], middle)
        updated = updated + extra_ref[pl.ds(i, 1), :]
        odd_ref[pl.ds(i, 1), :] = updated
        return updated

    lax.fori_loop(0, half, pair_step, prior_ref[...], unroll=2)
    prev_ref[0:1, :] = prior_ref[...]
    prev_ref[1:half, :] = odd_ref[0 : half - 1, :]
    predicted = times_transpose(prev_ref[...], transition)
    even_ref[...] = predicted + w_even * times_transpose(y_even - predicted, gain)
    own_rows(even_ref, odd_ref, own_ref)


def smooth_kernel(
    even_ref, odd_ref, a_ref, s_ref,
    s_even_ref, s_odd_ref, own_ref, u_ref, v_ref, t_ref, sq_ref, sq_t_ref,
):
    half = even_ref.shape[0]
    width = s_ref.shape[0]
    smoother = s_ref[...]
    transition = a_ref[...]
    for start in range(0, width, BAND):
        rows = slice(start, start + BAND)
        sq_ref[rows, :] = jnp.dot(s_ref[rows, :], smoother, preferred_element_type=F32)
    transpose_into(sq_t_ref, sq_ref)
    both = jnp.concatenate([even_ref[...], odd_ref[...]], axis=0)
    d_both = both - times_transpose(times_transpose(both, transition), smoother)
    d_even = d_both[:half]
    d_odd = d_both[half:]
    pulled = times_transpose(d_even, smoother)
    u_ref[0:1, :] = jnp.zeros((1, width), F32)
    u_ref[1:half, :] = pulled[1:half, :] + d_odd[0 : half - 1, :]
    twice = times_transpose(times_transpose(u_ref[...], smoother), smoother)
    v_ref[2:half, :] = twice[2:half, :] + u_ref[1 : half - 1, :]
    s_odd_ref[...] = jnp.zeros((half, width), F32)
    last = odd_ref[half - 1 : half, :]
    s_odd_ref[half - 1 : half, :] = last

    def quad_step(j, state):
        q = half - 1 - 2 * j
        middle = column_from_row(sq_ref[...], state)
        value = row_from_column(sq_t_ref[...], middle) + v_ref[pl.ds(q, 1), :]
        s_odd_ref[pl.ds(q - 2, 1), :] = value
        return value

    lax.fori_loop(0, half // 2 - 1, quad_step, last, unroll=2)
    odd_row = lax.broadcasted_iota(jnp.int32, (half, 1), 0) % 2 == 1
    first = times_transpose(s_odd_ref[...], smoother) + d_even
    s_even_ref[...] = jnp.where(odd_row, first, 0.0)
    t_ref[...] = times_transpose(s_even_ref[...], smoother)
    filled = t_ref[1:half, :] + d_odd[0 : half - 1, :]
    s_odd_ref[0 : half - 1, :] = jnp.where(odd_row[0 : half - 1], s_odd_ref[0 : half - 1, :], filled)
    third = times_transpose(s_odd_ref[...], smoother) + d_even
    s_even_ref[...] = jnp.where(odd_row, s_even_ref[...], third)
    own_rows(s_even_ref, s_odd_ref, own_ref)


VMEM_LIMIT = 60 * 1024 * 1024


def run_chain(weights, prior, transition, gain, smoother, observed):
    steps, width = observed.shape
    half = steps // 2
    vmem = pl.BlockSpec(memory_space=pltpu.VMEM)
    smem = pl.BlockSpec(memory_space=pltpu.SMEM)
    params = pltpu.CompilerParams(vmem_limit_bytes=VMEM_LIMIT)
    flags = weights.astype(jnp.int32)
    w_pair = weights.reshape(half, 2).T[:, :, None]
    y_pair = observed.reshape(half, 2, width).transpose(1, 0, 2)
    rows = jax.ShapeDtypeStruct((half, width), F32)
    square = pltpu.VMEM((width, width), F32)
    stacked = pltpu.VMEM((2, width, width), F32)
    seg = steps // lax.axis_size("tm")
    own = jax.ShapeDtypeStruct((seg, width // lax.axis_size("state")), F32)
    f_even, f_odd, f_own = pl.pallas_call(
        filter_kernel,
        out_shape=(rows, rows, own),
        in_specs=[smem] + [vmem] * 5,
        out_specs=(vmem, vmem, vmem),
        scratch_shapes=[pltpu.VMEM((half, width), F32)] * 2 + [stacked, stacked],
        compiler_params=params,
    )(flags, prior, w_pair, y_pair, transition, gain)
    _, _, s_own = pl.pallas_call(
        smooth_kernel,
        out_shape=(rows, rows, own),
        in_specs=[vmem] * 4,
        out_specs=(vmem, vmem, vmem),
        scratch_shapes=[pltpu.VMEM((half, width), F32)] * 3 + [square, square],
        compiler_params=params,
    )(f_even, f_odd, transition, smoother)
    return f_own, s_own


def gather_kernel(count, block_ref, out_ref, local_sem, send_sems, recv_sems, swap_sems):
    me = lax.axis_index("tm")
    lane = lax.axis_index("state")
    core = lax.rem(lane, 2)
    sibling = lane + 1 - 2 * core
    half = count // 2
    share = half - 1
    mesh_id = pl.DeviceIdType.MESH
    barrier = pltpu.get_barrier_semaphore()
    for step in range(1, count):
        peer = lax.rem(me + step, count)
        pl.semaphore_signal(barrier, inc=1, device_id={"tm": peer}, device_id_type=mesh_id)
    pl.semaphore_signal(barrier, inc=1, device_id={"state": sibling}, device_id_type=mesh_id)
    pl.semaphore_wait(barrier, count)

    def fetch(step):
        peer = lax.rem(me + step, count)
        return pltpu.make_async_remote_copy(
            src_ref=block_ref,
            dst_ref=out_ref.at[step],
            send_sem=send_sems.at[step],
            recv_sem=recv_sems.at[step],
            device_id={"tm": peer},
            device_id_type=mesh_id,
        )

    own = pltpu.make_async_copy(block_ref, out_ref.at[0], local_sem)

    @pl.when(core == 0)
    def _():
        own.start()

    copies = [fetch(core * share + j + 1) for j in range(share)]
    for copy in copies:
        copy.start()
    last = fetch(count - 1)

    @pl.when(core == 1)
    def _():
        last.start()

    for copy in copies:
        copy.wait()

    @pl.when(core == 1)
    def _():
        last.wait()

    @pl.when(core == 0)
    def _():
        own.wait()

    mine = pl.ds(core * half, half)
    swap = pltpu.make_async_remote_copy(
        src_ref=out_ref.at[mine],
        dst_ref=out_ref.at[mine],
        send_sem=swap_sems.at[0],
        recv_sem=swap_sems.at[1],
        device_id={"state": sibling},
        device_id_type=mesh_id,
    )
    swap.start()
    swap.wait()


def gather_over_time(block):
    count = lax.axis_size("tm")
    vmem = pl.BlockSpec(memory_space=pltpu.VMEM)
    return pl.pallas_call(
        functools.partial(gather_kernel, count),
        out_shape=jax.ShapeDtypeStruct((count,) + block.shape, block.dtype),
        in_specs=[vmem],
        out_specs=vmem,
        scratch_shapes=[
            pltpu.SemaphoreType.DMA,
            pltpu.SemaphoreType.DMA((count,)),
            pltpu.SemaphoreType.DMA((count,)),
            pltpu.SemaphoreType.DMA((2,)),
        ],
        compiler_params=pltpu.CompilerParams(collective_id=0, has_side_effects=True),
    )(block)


def local(prior, transition, gain, smoother, observed, present):
    panel = smoother.shape[0]
    seg, width = observed.shape
    count = lax.axis_size("tm")
    me = lax.axis_index("tm")
    dense = seg * width // 128
    flags = jnp.zeros((8, 128), F32).at[0, :seg].set(present.astype(F32))
    block = jnp.concatenate([observed.reshape(dense, 128), flags], axis=0)
    slots = gather_over_time(block)
    smoother, slots = lax.optimization_barrier((smoother, slots))
    order = lax.rem(me - jnp.arange(count) + count, count)
    slots = jnp.take(slots, order, axis=0)
    all_observed = slots[:, :dense, :].reshape(-1, width)
    weights = slots[:, dense, :seg].reshape(-1)
    smoother_full = lax.all_gather(smoother, "state", axis=0, tiled=True)
    f_own, s_own = run_chain(
        weights, prior[None, :], transition, gain, smoother_full, all_observed
    )
    return f_own, s_own


def solution(mesh):
    placed = (P(), P(), P(), P("state", None), P("tm", None), P("tm"))
    return jax.shard_map(
        local,
        mesh=mesh,
        in_specs=placed,
        out_specs=(P("tm", "state"), P("tm", "state")),
        check_vma=False,
    )
```

```python
import functools

import jax
import jax.numpy as jnp
from jax import lax
from jax.experimental import pallas as pl
from jax.experimental.pallas import tpu as pltpu
from jax.sharding import PartitionSpec as P

F32 = jnp.float32
BF16 = jnp.bfloat16
NT = (((1,), (1,)), ((), ()))


def pieces(x):
    hi = x.astype(BF16)
    rest = x - hi.astype(F32)
    mid = rest.astype(BF16)
    lo = (rest - mid.astype(F32)).astype(BF16)
    return hi, mid, lo


def times_transpose(rows, matrix):
    count = rows.shape[0]
    stacked = jnp.concatenate(pieces(rows), axis=0)
    out = lax.dot_general(stacked, matrix, NT, preferred_element_type=F32)
    return out[0:count] + out[count : 2 * count] + out[2 * count :]


def matvec_row(vector, matrix):
    hi, mid, lo = pieces(vector)
    width = vector.shape[1]
    row = lax.broadcasted_iota(jnp.int32, (8, width), 0)
    stacked = jnp.where(
        row == 0,
        hi.astype(F32),
        jnp.where(row == 1, mid.astype(F32), jnp.where(row == 2, lo.astype(F32), 0.0)),
    ).astype(BF16)
    out = lax.dot_general(stacked, matrix, NT, preferred_element_type=F32)
    return out[0:1] + out[1:2] + out[2:3]


def column_from_row(matrix, row):
    return jnp.sum(matrix * row, axis=1, keepdims=True)


def row_from_column(matrix_t, column):
    return jnp.sum(matrix_t * column, axis=0, keepdims=True)


BAND = 256


def transpose_into(dst, src):
    width = src.shape[0]
    for i in range(0, width, BAND):
        for j in range(0, width, BAND):
            dst[j : j + BAND, i : i + BAND] = src[i : i + BAND, j : j + BAND].T


def build_pairs(a_ref, g_ref, pair_ref, pair_t_ref):
    width = a_ref.shape[0]
    for start in range(0, width, BAND):
        rows = slice(start, start + BAND)
        a_rows = a_ref[rows, :].astype(F32)
        pair_ref[0, rows, :] = a_rows
        pair_ref[1, rows, :] = a_rows - jnp.dot(
            g_ref[rows, :], a_ref[...], preferred_element_type=F32
        )
    transpose_into(pair_t_ref.at[0], pair_ref.at[0])
    transpose_into(pair_t_ref.at[1], pair_ref.at[1])


def own_rows(even_ref, odd_ref, out_ref):
    per = out_ref.shape[0] // 2
    panel = out_ref.shape[1]
    width = even_ref.shape[1]
    base = lax.axis_index("tm") * per
    lane = lax.axis_index("state")
    rows = []
    for i in range(per):
        rows.append(even_ref[pl.ds(base + i, 1), :])
        rows.append(odd_ref[pl.ds(base + i, 1), :])
    block = jnp.concatenate(rows, axis=0)
    picked = block[:, 0:panel]
    for j in range(1, width // panel):
        picked = jnp.where(lane == j, block[:, j * panel : (j + 1) * panel], picked)
    out_ref[...] = picked


def filter_kernel(
    flag_ref, prior_ref, w_ref, y_ref, a_ref, g_ref,
    even_ref, odd_ref, own_ref, extra_ref, prev_ref, pair_ref, pair_t_ref,
):
    half = y_ref.shape[1]
    build_pairs(a_ref, g_ref, pair_ref, pair_t_ref)
    gain = g_ref[...]
    transition = a_ref[...]
    w_even, w_odd = w_ref[0], w_ref[1]
    y_even, y_odd = y_ref[0], y_ref[1]
    both = times_transpose(jnp.concatenate([y_even, y_odd], axis=0), gain)
    corr_even = w_even * both[:half]
    corr_odd = w_odd * both[half:]
    moved = times_transpose(corr_even, transition)
    extra_ref[...] = moved - w_odd * times_transpose(moved, gain) + corr_odd

    def pair_step(i, state):
        middle = column_from_row(pair_ref[flag_ref[2 * i]], state)
        updated = row_from_column(pair_t_ref[flag_ref[2 * i + 1]], middle)
        updated = updated + extra_ref[pl.ds(i, 1), :]
        odd_ref[pl.ds(i, 1), :] = updated
        return updated

    lax.fori_loop(0, half, pair_step, prior_ref[...], unroll=4)
    prev_ref[0:1, :] = prior_ref[...]
    prev_ref[1:half, :] = odd_ref[0 : half - 1, :]
    predicted = times_transpose(prev_ref[...], transition)
    even_ref[...] = predicted + w_even * times_transpose(y_even - predicted, gain)
    own_rows(even_ref, odd_ref, own_ref)


def smooth_kernel(
    even_ref, odd_ref, a_ref, s_ref,
    s_even_ref, s_odd_ref, own_ref, u_ref, v_ref, t_ref, sq_ref, sq_t_ref,
):
    half = even_ref.shape[0]
    width = s_ref.shape[0]
    smoother = s_ref[...]
    transition = a_ref[...]
    for start in range(0, width, BAND):
        rows = slice(start, start + BAND)
        sq_ref[rows, :] = jnp.dot(s_ref[rows, :], smoother, preferred_element_type=F32)
    transpose_into(sq_t_ref, sq_ref)
    both = jnp.concatenate([even_ref[...], odd_ref[...]], axis=0)
    d_both = both - times_transpose(times_transpose(both, transition), smoother)
    d_even = d_both[:half]
    d_odd = d_both[half:]
    pulled = times_transpose(d_even, smoother)
    u_ref[0:1, :] = jnp.zeros((1, width), F32)
    u_ref[1:half, :] = pulled[1:half, :] + d_odd[0 : half - 1, :]
    twice = times_transpose(times_transpose(u_ref[...], smoother), smoother)
    v_ref[2:half, :] = twice[2:half, :] + u_ref[1 : half - 1, :]
    s_odd_ref[...] = jnp.zeros((half, width), F32)
    last = odd_ref[half - 1 : half, :]
    s_odd_ref[half - 1 : half, :] = last

    def quad_step(j, state):
        q = half - 1 - 2 * j
        middle = column_from_row(sq_ref[...], state)
        value = row_from_column(sq_t_ref[...], middle) + v_ref[pl.ds(q, 1), :]
        s_odd_ref[pl.ds(q - 2, 1), :] = value
        return value

    lax.fori_loop(0, half // 2 - 1, quad_step, last, unroll=2)
    odd_row = lax.broadcasted_iota(jnp.int32, (half, 1), 0) % 2 == 1
    first = times_transpose(s_odd_ref[...], smoother) + d_even
    s_even_ref[...] = jnp.where(odd_row, first, 0.0)
    t_ref[...] = times_transpose(s_even_ref[...], smoother)
    filled = t_ref[1:half, :] + d_odd[0 : half - 1, :]
    s_odd_ref[0 : half - 1, :] = jnp.where(odd_row[0 : half - 1], s_odd_ref[0 : half - 1, :], filled)
    third = times_transpose(s_odd_ref[...], smoother) + d_even
    s_even_ref[...] = jnp.where(odd_row, s_even_ref[...], third)
    own_rows(s_even_ref, s_odd_ref, own_ref)


VMEM_LIMIT = 60 * 1024 * 1024


def run_chain(weights, prior, transition, gain, smoother, observed):
    steps, width = observed.shape
    half = steps // 2
    vmem = pl.BlockSpec(memory_space=pltpu.VMEM)
    smem = pl.BlockSpec(memory_space=pltpu.SMEM)
    params = pltpu.CompilerParams(vmem_limit_bytes=VMEM_LIMIT)
    flags = weights.astype(jnp.int32)
    w_pair = weights.reshape(half, 2).T[:, :, None]
    y_pair = observed.reshape(half, 2, width).transpose(1, 0, 2)
    rows = jax.ShapeDtypeStruct((half, width), F32)
    square = pltpu.VMEM((width, width), F32)
    stacked = pltpu.VMEM((2, width, width), F32)
    seg = steps // lax.axis_size("tm")
    own = jax.ShapeDtypeStruct((seg, width // lax.axis_size("state")), F32)
    f_even, f_odd, f_own = pl.pallas_call(
        filter_kernel,
        out_shape=(rows, rows, own),
        in_specs=[smem] + [vmem] * 5,
        out_specs=(vmem, vmem, vmem),
        scratch_shapes=[pltpu.VMEM((half, width), F32)] * 2 + [stacked, stacked],
        compiler_params=params,
    )(flags, prior, w_pair, y_pair, transition, gain)
    _, _, s_own = pl.pallas_call(
        smooth_kernel,
        out_shape=(rows, rows, own),
        in_specs=[vmem] * 4,
        out_specs=(vmem, vmem, vmem),
        scratch_shapes=[pltpu.VMEM((half, width), F32)] * 3 + [square, square],
        compiler_params=params,
    )(f_even, f_odd, transition, smoother)
    return f_own, s_own


def gather_kernel(count, block_ref, out_ref, local_sem, send_sems, recv_sems, swap_sems):
    me = lax.axis_index("tm")
    lane = lax.axis_index("state")
    core = lax.rem(lane, 2)
    sibling = lane + 1 - 2 * core
    half = count // 2
    share = half - 1
    mesh_id = pl.DeviceIdType.MESH
    barrier = pltpu.get_barrier_semaphore()
    for step in range(1, count):
        peer = lax.rem(me + step, count)
        pl.semaphore_signal(barrier, inc=1, device_id={"tm": peer}, device_id_type=mesh_id)
    pl.semaphore_signal(barrier, inc=1, device_id={"state": sibling}, device_id_type=mesh_id)
    pl.semaphore_wait(barrier, count)

    def fetch(step):
        peer = lax.rem(me + step, count)
        return pltpu.make_async_remote_copy(
            src_ref=block_ref,
            dst_ref=out_ref.at[step],
            send_sem=send_sems.at[step],
            recv_sem=recv_sems.at[step],
            device_id={"tm": peer},
            device_id_type=mesh_id,
        )

    own = pltpu.make_async_copy(block_ref, out_ref.at[0], local_sem)

    @pl.when(core == 0)
    def _():
        own.start()

    copies = [fetch(core * share + j + 1) for j in range(share)]
    for copy in copies:
        copy.start()
    last = fetch(count - 1)

    @pl.when(core == 1)
    def _():
        last.start()

    for copy in copies:
        copy.wait()

    @pl.when(core == 1)
    def _():
        last.wait()

    @pl.when(core == 0)
    def _():
        own.wait()

    mine = pl.ds(core * half, half)
    swap = pltpu.make_async_remote_copy(
        src_ref=out_ref.at[mine],
        dst_ref=out_ref.at[mine],
        send_sem=swap_sems.at[0],
        recv_sem=swap_sems.at[1],
        device_id={"state": sibling},
        device_id_type=mesh_id,
    )
    swap.start()
    swap.wait()


def gather_over_time(block):
    count = lax.axis_size("tm")
    vmem = pl.BlockSpec(memory_space=pltpu.VMEM)
    return pl.pallas_call(
        functools.partial(gather_kernel, count),
        out_shape=jax.ShapeDtypeStruct((count,) + block.shape, block.dtype),
        in_specs=[vmem],
        out_specs=vmem,
        scratch_shapes=[
            pltpu.SemaphoreType.DMA,
            pltpu.SemaphoreType.DMA((count,)),
            pltpu.SemaphoreType.DMA((count,)),
            pltpu.SemaphoreType.DMA((2,)),
        ],
        compiler_params=pltpu.CompilerParams(collective_id=0, has_side_effects=True),
    )(block)


def local(prior, transition, gain, smoother, observed, present):
    panel = smoother.shape[0]
    seg, width = observed.shape
    count = lax.axis_size("tm")
    me = lax.axis_index("tm")
    dense = seg * width // 128
    flags = jnp.zeros((8, 128), F32).at[0, :seg].set(present.astype(F32))
    block = jnp.concatenate([observed.reshape(dense, 128), flags], axis=0)
    slots = gather_over_time(block)
    smoother, slots = lax.optimization_barrier((smoother, slots))
    order = lax.rem(me - jnp.arange(count) + count, count)
    slots = jnp.take(slots, order, axis=0)
    all_observed = slots[:, :dense, :].reshape(-1, width)
    weights = slots[:, dense, :seg].reshape(-1)
    smoother_full = lax.all_gather(smoother, "state", axis=0, tiled=True)
    f_own, s_own = run_chain(
        weights, prior[None, :], transition, gain, smoother_full, all_observed
    )
    return f_own, s_own


def solution(mesh):
    placed = (P(), P(), P(), P("state", None), P("tm", None), P("tm"))
    return jax.shard_map(
        local,
        mesh=mesh,
        in_specs=placed,
        out_specs=(P("tm", "state"), P("tm", "state")),
        check_vma=False,
    )
```

```python
import functools

import jax
import jax.numpy as jnp
from jax import lax
from jax.experimental import pallas as pl
from jax.experimental.pallas import tpu as pltpu
from jax.sharding import PartitionSpec as P

F32 = jnp.float32
BF16 = jnp.bfloat16
NT = (((1,), (1,)), ((), ()))


def pieces(x):
    hi = x.astype(BF16)
    rest = x - hi.astype(F32)
    mid = rest.astype(BF16)
    lo = (rest - mid.astype(F32)).astype(BF16)
    return hi, mid, lo


def times_transpose(rows, matrix):
    count = rows.shape[0]
    stacked = jnp.concatenate(pieces(rows), axis=0)
    out = lax.dot_general(stacked, matrix, NT, preferred_element_type=F32)
    return out[0:count] + out[count : 2 * count] + out[2 * count :]


def matvec_row(vector, matrix):
    hi, mid, lo = pieces(vector)
    width = vector.shape[1]
    row = lax.broadcasted_iota(jnp.int32, (8, width), 0)
    stacked = jnp.where(
        row == 0,
        hi.astype(F32),
        jnp.where(row == 1, mid.astype(F32), jnp.where(row == 2, lo.astype(F32), 0.0)),
    ).astype(BF16)
    out = lax.dot_general(stacked, matrix, NT, preferred_element_type=F32)
    return out[0:1] + out[1:2] + out[2:3]


def column_from_row(matrix, row):
    return jnp.sum(matrix * row, axis=1, keepdims=True)


def row_from_column(matrix_t, column):
    return jnp.sum(matrix_t * column, axis=0, keepdims=True)


BAND = 256


def transpose_into(dst, src):
    width = src.shape[0]
    for i in range(0, width, BAND):
        for j in range(0, width, BAND):
            dst[j : j + BAND, i : i + BAND] = src[i : i + BAND, j : j + BAND].T


def build_pairs(a_ref, g_ref, pair_ref, pair_t_ref):
    width = a_ref.shape[0]
    for start in range(0, width, BAND):
        rows = slice(start, start + BAND)
        a_rows = a_ref[rows, :].astype(F32)
        pair_ref[0, rows, :] = a_rows
        pair_ref[1, rows, :] = a_rows - jnp.dot(
            g_ref[rows, :], a_ref[...], preferred_element_type=F32
        )
    transpose_into(pair_t_ref.at[0], pair_ref.at[0])
    transpose_into(pair_t_ref.at[1], pair_ref.at[1])


def own_rows(even_ref, odd_ref, out_ref):
    per = out_ref.shape[0] // 2
    panel = out_ref.shape[1]
    width = even_ref.shape[1]
    base = lax.axis_index("tm") * per
    lane = lax.axis_index("state")
    rows = []
    for i in range(per):
        rows.append(even_ref[pl.ds(base + i, 1), :])
        rows.append(odd_ref[pl.ds(base + i, 1), :])
    block = jnp.concatenate(rows, axis=0)
    picked = block[:, 0:panel]
    for j in range(1, width // panel):
        picked = jnp.where(lane == j, block[:, j * panel : (j + 1) * panel], picked)
    out_ref[...] = picked


def filter_kernel(
    flag_ref, prior_ref, w_ref, y_ref, a_ref, g_ref,
    even_ref, odd_ref, own_ref, extra_ref, prev_ref, pair_ref, pair_t_ref,
):
    half = y_ref.shape[1]
    build_pairs(a_ref, g_ref, pair_ref, pair_t_ref)
    gain = g_ref[...]
    transition = a_ref[...]
    w_even, w_odd = w_ref[0], w_ref[1]
    y_even, y_odd = y_ref[0], y_ref[1]
    both = times_transpose(jnp.concatenate([y_even, y_odd], axis=0), gain)
    corr_even = w_even * both[:half]
    corr_odd = w_odd * both[half:]
    moved = times_transpose(corr_even, transition)
    extra_ref[...] = moved - w_odd * times_transpose(moved, gain) + corr_odd

    def pair_step(i, state):
        middle = column_from_row(pair_ref[flag_ref[2 * i].astype(jnp.int32)], state)
        updated = row_from_column(pair_t_ref[flag_ref[2 * i + 1].astype(jnp.int32)], middle)
        updated = updated + extra_ref[pl.ds(i, 1), :]
        odd_ref[pl.ds(i, 1), :] = updated
        return updated

    lax.fori_loop(0, half, pair_step, prior_ref[...], unroll=2)
    prev_ref[0:1, :] = prior_ref[...]
    prev_ref[1:half, :] = odd_ref[0 : half - 1, :]
    predicted = times_transpose(prev_ref[...], transition)
    even_ref[...] = predicted + w_even * times_transpose(y_even - predicted, gain)
    own_rows(even_ref, odd_ref, own_ref)


def smooth_kernel(
    even_ref, odd_ref, a_ref, s_ref,
    s_even_ref, s_odd_ref, own_ref, u_ref, v_ref, t_ref, sq_ref, sq_t_ref,
):
    half = even_ref.shape[0]
    width = s_ref.shape[0]
    smoother = s_ref[...]
    transition = a_ref[...]
    for start in range(0, width, BAND):
        rows = slice(start, start + BAND)
        sq_ref[rows, :] = jnp.dot(s_ref[rows, :], smoother, preferred_element_type=F32)
    transpose_into(sq_t_ref, sq_ref)
    both = jnp.concatenate([even_ref[...], odd_ref[...]], axis=0)
    d_both = both - times_transpose(times_transpose(both, transition), smoother)
    d_even = d_both[:half]
    d_odd = d_both[half:]
    pulled = times_transpose(d_even, smoother)
    u_ref[0:1, :] = jnp.zeros((1, width), F32)
    u_ref[1:half, :] = pulled[1:half, :] + d_odd[0 : half - 1, :]
    twice = times_transpose(times_transpose(u_ref[...], smoother), smoother)
    v_ref[2:half, :] = twice[2:half, :] + u_ref[1 : half - 1, :]
    s_odd_ref[...] = jnp.zeros((half, width), F32)
    last = odd_ref[half - 1 : half, :]
    s_odd_ref[half - 1 : half, :] = last

    def quad_step(j, state):
        q = half - 1 - 2 * j
        middle = column_from_row(sq_ref[...], state)
        value = row_from_column(sq_t_ref[...], middle) + v_ref[pl.ds(q, 1), :]
        s_odd_ref[pl.ds(q - 2, 1), :] = value
        return value

    lax.fori_loop(0, half // 2 - 1, quad_step, last, unroll=2)
    odd_row = lax.broadcasted_iota(jnp.int32, (half, 1), 0) % 2 == 1
    first = times_transpose(s_odd_ref[...], smoother) + d_even
    s_even_ref[...] = jnp.where(odd_row, first, 0.0)
    t_ref[...] = times_transpose(s_even_ref[...], smoother)
    filled = t_ref[1:half, :] + d_odd[0 : half - 1, :]
    s_odd_ref[0 : half - 1, :] = jnp.where(odd_row[0 : half - 1], s_odd_ref[0 : half - 1, :], filled)
    third = times_transpose(s_odd_ref[...], smoother) + d_even
    s_even_ref[...] = jnp.where(odd_row, s_even_ref[...], third)
    own_rows(s_even_ref, s_odd_ref, own_ref)


VMEM_LIMIT = 60 * 1024 * 1024


def run_chain(weights, prior, transition, gain, smoother, observed):
    steps, width = observed.shape
    half = steps // 2
    vmem = pl.BlockSpec(memory_space=pltpu.VMEM)
    smem = pl.BlockSpec(memory_space=pltpu.SMEM)
    params = pltpu.CompilerParams(vmem_limit_bytes=VMEM_LIMIT)
    flags = weights
    w_pair = weights.reshape(half, 2).T[:, :, None]
    y_pair = observed.reshape(half, 2, width).transpose(1, 0, 2)
    rows = jax.ShapeDtypeStruct((half, width), F32)
    square = pltpu.VMEM((width, width), F32)
    stacked = pltpu.VMEM((2, width, width), F32)
    seg = steps // lax.axis_size("tm")
    own = jax.ShapeDtypeStruct((seg, width // lax.axis_size("state")), F32)
    f_even, f_odd, f_own = pl.pallas_call(
        filter_kernel,
        out_shape=(rows, rows, own),
        in_specs=[smem] + [vmem] * 5,
        out_specs=(vmem, vmem, vmem),
        scratch_shapes=[pltpu.VMEM((half, width), F32)] * 2 + [stacked, stacked],
        compiler_params=params,
    )(flags, prior, w_pair, y_pair, transition, gain)
    _, _, s_own = pl.pallas_call(
        smooth_kernel,
        out_shape=(rows, rows, own),
        in_specs=[vmem] * 4,
        out_specs=(vmem, vmem, vmem),
        scratch_shapes=[pltpu.VMEM((half, width), F32)] * 3 + [square, square],
        compiler_params=params,
    )(f_even, f_odd, transition, smoother)
    return f_own, s_own


def gather_kernel(count, block_ref, out_ref, local_sem, send_sems, recv_sems, swap_sems):
    me = lax.axis_index("tm")
    lane = lax.axis_index("state")
    core = lax.rem(lane, 2)
    sibling = lane + 1 - 2 * core
    half = count // 2
    share = half - 1
    mesh_id = pl.DeviceIdType.MESH
    barrier = pltpu.get_barrier_semaphore()
    for step in range(1, count):
        peer = lax.rem(me + step, count)
        pl.semaphore_signal(barrier, inc=1, device_id={"tm": peer}, device_id_type=mesh_id)
    pl.semaphore_signal(barrier, inc=1, device_id={"state": sibling}, device_id_type=mesh_id)
    pl.semaphore_wait(barrier, count)

    def fetch(step):
        peer = lax.rem(me + step, count)
        return pltpu.make_async_remote_copy(
            src_ref=block_ref,
            dst_ref=out_ref.at[step],
            send_sem=send_sems.at[step],
            recv_sem=recv_sems.at[step],
            device_id={"tm": peer},
            device_id_type=mesh_id,
        )

    own = pltpu.make_async_copy(block_ref, out_ref.at[0], local_sem)

    @pl.when(core == 0)
    def _():
        own.start()

    copies = [fetch(core * share + j + 1) for j in range(share)]
    for copy in copies:
        copy.start()
    last = fetch(count - 1)

    @pl.when(core == 1)
    def _():
        last.start()

    for copy in copies:
        copy.wait()

    @pl.when(core == 1)
    def _():
        last.wait()

    @pl.when(core == 0)
    def _():
        own.wait()

    mine = pl.ds(core * half, half)
    swap = pltpu.make_async_remote_copy(
        src_ref=out_ref.at[mine],
        dst_ref=out_ref.at[mine],
        send_sem=swap_sems.at[0],
        recv_sem=swap_sems.at[1],
        device_id={"state": sibling},
        device_id_type=mesh_id,
    )
    swap.start()
    swap.wait()


def gather_over_time(block):
    count = lax.axis_size("tm")
    vmem = pl.BlockSpec(memory_space=pltpu.VMEM)
    return pl.pallas_call(
        functools.partial(gather_kernel, count),
        out_shape=jax.ShapeDtypeStruct((count,) + block.shape, block.dtype),
        in_specs=[vmem],
        out_specs=vmem,
        scratch_shapes=[
            pltpu.SemaphoreType.DMA,
            pltpu.SemaphoreType.DMA((count,)),
            pltpu.SemaphoreType.DMA((count,)),
            pltpu.SemaphoreType.DMA((2,)),
        ],
        compiler_params=pltpu.CompilerParams(collective_id=0, has_side_effects=True),
    )(block)


def local(prior, transition, gain, smoother, observed, present):
    panel = smoother.shape[0]
    seg, width = observed.shape
    count = lax.axis_size("tm")
    me = lax.axis_index("tm")
    dense = seg * width // 128
    flags = jnp.zeros((8, 128), F32).at[0, :seg].set(present.astype(F32))
    block = jnp.concatenate([observed.reshape(dense, 128), flags], axis=0)
    slots = gather_over_time(block)
    smoother, slots = lax.optimization_barrier((smoother, slots))
    order = lax.rem(me - jnp.arange(count) + count, count)
    slots = jnp.take(slots, order, axis=0)
    all_observed = slots[:, :dense, :].reshape(-1, width)
    weights = slots[:, dense, :seg].reshape(-1)
    smoother_full = lax.all_gather(smoother, "state", axis=0, tiled=True)
    f_own, s_own = run_chain(
        weights, prior[None, :], transition, gain, smoother_full, all_observed
    )
    return f_own, s_own


def solution(mesh):
    placed = (P(), P(), P(), P("state", None), P("tm", None), P("tm"))
    return jax.shard_map(
        local,
        mesh=mesh,
        in_specs=placed,
        out_specs=(P("tm", "state"), P("tm", "state")),
        check_vma=False,
    )
```
